512 devices in a mesh: tm: 128 (over z, y, core), zone: 4 (over x).
Axes of the slice: x: 4, y: 8, z: 8, core: 2. Of those that a mesh axis runs over, the one named last changes fastest.
Arguments:
- source_field: float32 [1024, 8192], P('tm', 'zone'), may hold values from -6 to 6
- remap_weights: bfloat16 [64, 8, 128, 128], P('zone'), may hold values from -0.1875 to 0.1875
- block_columns: int32 [64, 8], P('zone'), may hold values from 0 to 63, all different within a row
- piece_sizes: int32 [4, 128], P('zone'), may hold values from 1 to 64, 2048 in all within a row
- filter_taps: float32 [1023], replicated, may hold values from -0.1875 to 0.1875
Outputs:
- adjoint_field: float32 [1024, 8192], P('tm', 'zone')
The draws below stay inside these ranges and needn't reach their ends.
Inputs may be any that keep to these rules, and one draw needn't show every extreme that they name: `block_columns`: the 8 source blocks of one target block are distinct; every source block feeds some target block. `piece_sizes`: each row sums to 2048; its largest basin has exactly 64 cells.
All inputs are finite; a program needn't handle non-finite values.
Results may differ from the reference program's by a relative error of at most 0.0038.
Values may be sent and summed in bfloat16 or wider, within the bound.
A program may use at most 64 MiB of HBM per device.

```python
import math
import jax
import jax.numpy as jnp
import numpy as np
from jax import lax

BS = 128
KB = 8
NB = 64
NC = 8192
NCZ = 2048
SNAPS = 1024
TAPS = 1023
MOST = 64
N_TM = 128
N_ZONE = 4


def block_levels(stream_key, shape, cuts, least, top_value):
    gain = 1.0
    for axis_at, parts in cuts:
        heights = jax.random.uniform(jax.random.fold_in(jax.random.fold_in(stream_key, 6), axis_at), (parts,), jnp.float32, least / len(cuts), top_value / len(cuts))
        gain = gain * jnp.repeat(jnp.exp(heights), shape[axis_at] // parts).reshape((-1,) + (1,) * (len(shape) - 1 - axis_at))
    return gain


def picks_of(own_key, rows, count, top, lift):
    order = jax.random.permutation(jax.random.fold_in(own_key, 1), count)
    pull = order
    for power in range(3):
        pull = pull * pull // count
    pull = pull * lift // count
    tickets = jax.random.randint(jax.random.fold_in(own_key, 2), (rows, count), 0, 4096) + pull
    sure = jax.random.permutation(jax.random.fold_in(own_key, 3), rows)[jnp.arange(count) % rows]
    tickets = jnp.where(jnp.arange(rows)[:, None] == sure[None, :], 1 << 14, tickets)
    merit = tickets * count + jnp.arange(count)
    return lax.top_k(merit.astype(jnp.int32), top)[1].astype(jnp.int32)


def profile(amount, total, limit, lean):
    weights = [(1 << 20) // math.isqrt(grade ** lean) + 1 for grade in range(2, amount + 1)]
    rest, counts = total - limit - (amount - 1), [1] * (amount - 1)
    while rest > 0:
        candidates = [i for i in range(amount - 1) if counts[i] < limit]
        pool, budget = sum([weights[i] for i in candidates]), rest
        for i in candidates:
            extra = min(limit - counts[i], max(1, budget * weights[i] // pool), rest)
            counts[i] = counts[i] + extra
            rest = rest - extra
    return np.array([limit] + counts)


def uneven_parts(stream_key, number_of, total, bound, slope):
    if number_of == 2:
        one = jax.random.randint(stream_key, (), max(1, total - bound), min(bound, total - 1) + 1)
        return jnp.stack([one, total - one])
    tallies = jnp.asarray(profile(number_of, total, bound, slope), jnp.int32)
    twos = (number_of - 1) // 2
    giver, sink = tallies[1:1 + 2 * twos:2], tallies[2:2 + 2 * twos:2]
    margin = jnp.minimum(giver - 1, bound - sink)
    passed = jax.random.randint(jax.random.fold_in(stream_key, 1), (twos,), 0, 1 << 20) % (margin + 1)
    tallies = tallies.at[1:1 + 2 * twos:2].set(giver - passed).at[2:2 + 2 * twos:2].set(sink + passed)
    return tallies[jax.random.permutation(jax.random.fold_in(stream_key, 2), number_of)]


def centred(stream_key, dims, scale, limit, split=(), held_as=jnp.bfloat16):
    entries = scale * jax.random.normal(stream_key, dims, jnp.float32)
    if split:
        entries = entries * block_levels(stream_key, dims, split, -0.22, 0.18)
    return jnp.clip(entries, -limit, limit).astype(held_as)


def setup_inputs(seed: int = 0) -> dict:
    arg_keys = jax.random.split(jax.random.key(seed), 6)
    source_field = centred(arg_keys[0], (SNAPS, NC), 1.0, 6.0, ((0, 128), (1, 4)), jnp.float32)
    remap_weights = centred(arg_keys[1], (NB, KB, BS, BS), (KB * BS) ** -0.5, 0.1875, ((0, 4),))
    block_columns = picks_of(arg_keys[2], NB, NB, KB, 0)
    piece_sizes = jax.vmap(lambda own: uneven_parts(own, N_TM, NCZ, MOST, 2))(jax.random.split(arg_keys[3], N_ZONE)).reshape((N_ZONE, N_TM)).astype(jnp.int32)
    filter_taps = centred(arg_keys[4], (TAPS,), TAPS ** -0.5, 0.1875, (), jnp.float32)
    return dict(source_field=source_field, remap_weights=remap_weights, block_columns=block_columns, piece_sizes=piece_sizes, filter_taps=filter_taps)


def toeplitz_rows(filter_taps, block_rows, span):
    tap_count = filter_taps.shape[0]
    extended = jnp.concatenate([filter_taps, jnp.zeros((span + 1 - tap_count,), filter_taps.dtype)])
    flat = jnp.broadcast_to(extended[None, :], (block_rows, span + 1)).reshape(block_rows * (span + 1))
    return flat[:block_rows * span].reshape(block_rows, span)


def banded(series, filter_taps):
    length, breadth = series.shape
    tap_count = filter_taps.shape[0]
    half_width = (tap_count - 1) // 2
    block_rows = min(512, length)
    toeplitz = toeplitz_rows(filter_taps, block_rows, block_rows + 2 * half_width)
    padded = jnp.pad(series, ((half_width, half_width), (0, 0)))

    def one_block(start):
        window = lax.dynamic_slice_in_dim(padded, start, block_rows + 2 * half_width, 0)
        return jnp.dot(toeplitz, window, precision=lax.Precision.HIGHEST, preferred_element_type=series.dtype)

    starts = (jnp.arange(length // block_rows) * block_rows).astype(jnp.int32)
    return lax.map(one_block, starts).reshape(length, breadth)


def remove_mean(stress, sizes_row):
    cells = stress.shape[1]
    ends = jnp.cumsum(sizes_row)
    begins = ends - sizes_row
    cell_ids = jnp.arange(cells, dtype=jnp.int32)[:, None]
    member = ((cell_ids >= begins[None, :]) & (cell_ids < ends[None, :])).astype(stress.dtype)
    totals = jnp.dot(stress, member, precision=lax.Precision.HIGHEST)
    means = totals / sizes_row.astype(stress.dtype)[None, :]
    return stress - jnp.dot(means, member.T, precision=lax.Precision.HIGHEST)


def reference(source_field, remap_weights, block_columns, piece_sizes, filter_taps):
    xlow = source_field.astype(jnp.bfloat16)
    blocks = xlow.astype(jnp.float32).reshape(SNAPS, NB, BS)

    def forward_row(index):
        picked = blocks[:, block_columns[index]]
        return jnp.einsum("tkb,kab->ta", picked, remap_weights[index].astype(jnp.float32))

    wind = jnp.transpose(lax.map(forward_row, jnp.arange(NB, dtype=jnp.int32)), (1, 0, 2)).reshape(SNAPS, NC)
    stress = wind * jnp.abs(wind)
    pieces = []
    for zone_id in range(N_ZONE):
        part_cells = stress[:, zone_id * NCZ:(zone_id + 1) * NCZ]
        pieces.append(remove_mean(part_cells, piece_sizes[zone_id]))
    anomaly = jnp.concatenate(pieces, axis=1)
    filtered = banded(anomaly, filter_taps)
    flow_low = filtered.astype(jnp.bfloat16).astype(jnp.float32).reshape(SNAPS, NB, BS)

    def backward_row(total, index):
        contrib = jnp.einsum("ta,kab->tkb", flow_low[:, index], remap_weights[index].astype(jnp.float32))
        return total.at[:, block_columns[index]].add(contrib), None

    start_total = jnp.zeros((SNAPS, NB, BS), jnp.float32)
    total, unused = lax.scan(backward_row, start_total, jnp.arange(NB, dtype=jnp.int32))
    return total.reshape(SNAPS, NC)
```

```python
import functools

import jax
import jax.numpy as jnp
from jax import lax
from jax.experimental import pallas as pl
from jax.experimental.pallas import tpu as pltpu
from jax.sharding import PartitionSpec as P

MESH = pl.DeviceIdType.MESH
F32 = jnp.float32
BF16 = jnp.bfloat16
SNAP = 8
LANE = 128
BLOCKS = 16
SLOTS = 8
ROWS = 4


def iota(shape, dim):
    return lax.broadcasted_iota(jnp.int32, shape, dim)


def two_parts(value):
    high = value.astype(BF16)
    low = (value - high.astype(F32)).astype(BF16)
    return high, low


def ring_distance(offset, length):
    return min(offset, length - offset)


def plane_offsets(rings, ring, cores):
    span = ring * cores
    offsets = [(dz, dq) for dz in range(rings) for dq in range(span)]
    offsets.remove((0, 0))

    def hops(offset):
        dz, dq = offset
        return ring_distance(dz, rings) + ring_distance(dq // cores, ring)

    return sorted(offsets, key=lambda offset: -hops(offset))


def kernel(
    n_tm,
    n_zone,
    source,
    weights,
    columns,
    sizes,
    taps,
    out,
    x_in,
    x_all,
    w_all,
    cols,
    toeplitz,
    members,
    send_a,
    recv_a,
    send_b,
    recv_b,
    contrib,
    part_out,
    part_in,
    part_own,
    arranged,
    load_sem,
    x_send,
    x_recv,
    a_send,
    a_recv,
    b_send,
    b_recv,
    p_send,
    p_recv,
):
    tm = lax.axis_index("tm")
    zone = lax.axis_index("zone")
    rings, ring, cores = 8, 8, 2
    span = ring * cores
    tz, tq = tm // span, lax.rem(tm, span)
    others = []
    for dz, dq in plane_offsets(rings, ring, cores):
        others.append(lax.rem(tz + dz, rings) * span + lax.rem(tq + dq, span))
    zones = [lax.rem(zone + step, n_zone) for step in (2, 1, 3)]

    barrier = pltpu.get_barrier_semaphore()
    for peer in others:
        pl.semaphore_signal(barrier, inc=1, device_id={"tm": peer}, device_id_type=MESH)
    for peer in zones:
        pl.semaphore_signal(barrier, inc=1, device_id={"zone": peer}, device_id_type=MESH)

    load_x = pltpu.make_async_copy(source, x_in, load_sem.at[0])
    load_c = pltpu.make_async_copy(columns, cols, load_sem.at[1])
    load_w = pltpu.make_async_copy(weights, w_all, load_sem.at[2])
    load_x.start()
    load_c.start()
    load_w.start()

    tap_rows = taps[...]
    pieces = []
    for q in range(8):
        row = jnp.broadcast_to(tap_rows[q : q + 1, :], (8, LANE))
        pieces.append(jnp.where(lax.rem(iota((8, LANE), 1), 8) == iota((8, LANE), 0), row, 0.0))
    spread = jnp.concatenate(pieces, axis=1)
    pick = (iota((1024, LANE), 0) // 8 == iota((1024, LANE), 1)).astype(BF16)
    top, rest = two_parts(spread)
    last = (spread - top.astype(F32) - rest.astype(F32)).astype(BF16)
    by_phase = (
        jnp.dot(top, pick, preferred_element_type=F32)
        + jnp.dot(rest, pick, preferred_element_type=F32)
        + jnp.dot(last, pick, preferred_element_type=F32)
    )
    for n in range(15):
        phase, shift = (n, 63) if n < 8 else (n - 8, 64)
        line = jnp.concatenate([by_phase[phase : phase + 1, :], jnp.zeros((1, LANE), F32)], axis=1)
        wide = jnp.broadcast_to(line, (LANE, 2 * LANE))
        rolled = pltpu.roll(wide, 256 - shift, 1, stride=1, stride_axis=0)[:, :LANE]
        high, low = two_parts(rolled)
        toeplitz[n * LANE : (n + 1) * LANE, :LANE] = high
        toeplitz[n * LANE : (n + 1) * LANE, LANE:] = low

    size_row = sizes[...].astype(F32)
    size_wide = jnp.broadcast_to(size_row, (LANE, LANE))
    upto = jnp.sum(
        jnp.where(iota((LANE, LANE), 1) <= iota((LANE, LANE), 0), size_wide, 0.0), axis=1, keepdims=True
    )
    before = jnp.sum(
        jnp.where(iota((LANE, LANE), 1) < iota((LANE, LANE), 0), size_wide, 0.0), axis=1, keepdims=True
    )
    for i in range(BLOCKS):
        cell = (iota((LANE, LANE), 1) + i * LANE).astype(F32)
        inside = (cell >= before) & (cell < upto)
        members[:, i * LANE : (i + 1) * LANE] = inside.astype(BF16)

    load_x.wait()
    for i in range(BLOCKS):
        x_all[zone * BLOCKS + i] = x_in[:, i * LANE : (i + 1) * LANE].astype(BF16)
    pl.semaphore_wait(barrier, n_tm - 1 + n_zone - 1)
    mine = x_all.at[pl.ds(zone * BLOCKS, BLOCKS)]
    x_copies = []
    for n, peer in enumerate(zones):
        x_copies.append(
            pltpu.make_async_remote_copy(
                src_ref=mine,
                dst_ref=mine,
                send_sem=x_send.at[n],
                recv_sem=x_recv.at[n],
                device_id={"zone": peer},
                device_id_type=MESH,
            )
        )
        x_copies[-1].start()
    load_c.wait()
    load_w.wait()
    for copy in x_copies:
        copy.wait_recv()

    stress = []
    for i in range(BLOCKS):
        wind = jnp.zeros((SNAP, LANE), F32)
        for k in range(0, SLOTS, 2):
            x_pair = jnp.concatenate([x_all[cols[i, k]], x_all[cols[i, k + 1]]], axis=1)
            w_pair = jnp.concatenate([w_all[i, k], w_all[i, k + 1]], axis=1)
            wind += lax.dot_general(
                x_pair, w_pair, (((1,), (1,)), ((), ())), preferred_element_type=F32
            )
        stress.append(wind * jnp.abs(wind))

    wide = jnp.concatenate(stress, axis=1)
    high, low = two_parts(wide)
    member = members[...]
    both = jnp.concatenate([high, low], axis=0)
    totals = lax.dot_general(both, member, (((1,), (1,)), ((), ())), preferred_element_type=F32)
    means = (totals[:SNAP] + totals[SNAP:]) / size_row
    high, low = two_parts(means)
    both = jnp.concatenate([high, low], axis=0)
    spread = jnp.dot(both, member, preferred_element_type=F32)
    anomaly = wide - spread[:SNAP] - spread[SNAP:]
    tiles = jnp.concatenate([anomaly[:, i * LANE : (i + 1) * LANE] for i in range(BLOCKS)], axis=0)

    def exchange(send, recv, send_sem, recv_sem):
        recv[pl.ds(tm, 1)] = send[pl.ds(tm, 1)]
        for peer in others:
            pltpu.make_async_remote_copy(
                src_ref=send.at[pl.ds(peer, 1)],
                dst_ref=recv.at[pl.ds(tm, 1)],
                send_sem=send_sem,
                recv_sem=recv_sem,
                device_id={"tm": peer},
                device_id_type=MESH,
            ).start()

    def rows_wait(ref, sem):
        rows = ref.at[pl.ds(0, n_tm - 1)]
        pltpu.make_async_copy(rows, rows, sem).wait()

    send_a[...] = tiles.T.reshape(n_tm, 1, LANE)
    exchange(send_a, recv_a, a_send, a_recv)
    rows_wait(recv_a, a_recv)

    series = recv_a[...].reshape(n_tm, LANE)
    high, low = two_parts(series)
    upper = jnp.concatenate([high, low], axis=1)
    lower = jnp.concatenate([high, jnp.zeros_like(high)], axis=1)
    right = jnp.concatenate([upper, lower], axis=0)
    phase = lax.rem(iota((n_tm, LANE), 1), 8)
    filtered = jnp.zeros((n_tm, LANE), F32)
    for n in range(15):
        k = n - 7
        product = jnp.dot(toeplitz[n * LANE : (n + 1) * LANE, :], right, preferred_element_type=F32)
        product = product[:, :LANE] + product[:, LANE:]
        moved = product if k == 0 else pltpu.roll(product, (-k) % LANE, 1)
        filtered += jnp.where((phase + k >= 0) & (phase + k < 8), moved, 0.0)
    send_b[...] = filtered.reshape(n_tm, 1, LANE)
    exchange(send_b, recv_b, b_send, b_recv)
    rows_wait(recv_b, b_recv)

    flow = recv_b[...].reshape(n_tm, LANE).T.astype(BF16)
    for i in range(BLOCKS):
        left = flow[i * SNAP : (i + 1) * SNAP, :]
        for k in range(0, SLOTS, 2):
            w_pair = jnp.concatenate([w_all[i, k], w_all[i, k + 1]], axis=1)
            pair = jnp.dot(left, w_pair, preferred_element_type=F32)
            base = (i * SLOTS + k) * SNAP
            contrib[base : base + SNAP, :] = pair[:, :LANE]
            contrib[base + SNAP : base + 2 * SNAP, :] = pair[:, LANE:]
    n_pairs = BLOCKS * SLOTS
    all_blocks = BLOCKS * n_zone
    column_row = jnp.zeros((1, LANE), jnp.int32)
    lane = iota((1, LANE), 1)
    for i in range(BLOCKS):
        for k in range(SLOTS):
            column_row = jnp.where(lane == i * SLOTS + k, cols[i, k], column_row)
    chosen = (iota((all_blocks, LANE), 0) == column_row).astype(BF16)
    chosen = jnp.concatenate([chosen, chosen], axis=1)
    sums = []
    for t in range(0, SNAP, 2):
        sides = []
        for side in (t, t + 1):
            high, low = two_parts(contrib[pl.ds(side, n_pairs, stride=SNAP), :])
            sides.append(jnp.concatenate([high, low], axis=0))
        both = jnp.dot(chosen, jnp.concatenate(sides, axis=1), preferred_element_type=F32)
        sums += [both[:, :LANE], both[:, LANE:]]
    for t in range(SNAP):
        for z in range(n_zone):
            part = sums[t][z * BLOCKS : (z + 1) * BLOCKS]
            part_out[z, t] = part.astype(BF16)
            part_own[z, t] = part
    p_copies = []
    for n, peer in enumerate(zones):
        p_copies.append(
            pltpu.make_async_remote_copy(
                src_ref=part_out.at[peer],
                dst_ref=part_in.at[n],
                send_sem=p_send.at[n],
                recv_sem=p_recv.at[n],
                device_id={"zone": peer},
                device_id_type=MESH,
            )
        )
        p_copies[-1].start()
    for copy in p_copies:
        copy.wait_recv()
    for t in range(SNAP):
        total = part_own[zone, t]
        for n in range(n_zone - 1):
            total += part_in[n, t].astype(F32)
        arranged[pl.ds(t, BLOCKS, stride=SNAP), :] = total
    for i in range(BLOCKS):
        out[:, i * LANE : (i + 1) * LANE] = arranged[i * SNAP : (i + 1) * SNAP, :]
    for copy in x_copies + p_copies:
        copy.wait_send()
    rows_wait(send_a, a_send)
    rows_wait(send_b, b_send)


def solution(mesh):
    n_tm, n_zone = mesh.shape["tm"], mesh.shape["zone"]

    def shards(source_field, remap_weights, block_columns, piece_sizes, filter_taps):
        taps = jnp.pad(filter_taps, (0, 1)).reshape(8, LANE)
        any_space = pl.BlockSpec(memory_space=pl.ANY)
        vmem = pl.BlockSpec(memory_space=pltpu.VMEM)
        dma = pltpu.SemaphoreType.DMA
        return pl.pallas_call(
            functools.partial(kernel, n_tm, n_zone),
            name="flux",
            out_shape=jax.ShapeDtypeStruct(source_field.shape, F32),
            in_specs=[any_space, any_space, any_space, vmem, vmem],
            out_specs=vmem,
            scratch_shapes=[
                pltpu.VMEM(source_field.shape, F32),
                pltpu.VMEM((BLOCKS * n_zone, SNAP, LANE), BF16),
                pltpu.VMEM(remap_weights.shape, BF16),
                pltpu.SMEM(block_columns.shape, jnp.int32),
                pltpu.VMEM((15 * LANE, 2 * LANE), BF16),
                pltpu.VMEM((LANE, BLOCKS * LANE), BF16),
                pltpu.VMEM((n_tm, 1, LANE), F32),
                pltpu.VMEM((n_tm, 1, LANE), F32),
                pltpu.VMEM((n_tm, 1, LANE), F32),
                pltpu.VMEM((n_tm, 1, LANE), F32),
                pltpu.VMEM((BLOCKS * SLOTS * SNAP, LANE), F32),
                pltpu.VMEM((n_zone, SNAP, BLOCKS, LANE), BF16),
                pltpu.VMEM((n_zone - 1, SNAP, BLOCKS, LANE), BF16),
                pltpu.VMEM((n_zone, SNAP, BLOCKS, LANE), F32),
                pltpu.VMEM((BLOCKS * SNAP, LANE), F32),
                dma((3,)),
                dma((n_zone - 1,)),
                dma((n_zone - 1,)),
                dma,
                dma,
                dma,
                dma,
                dma((n_zone - 1,)),
                dma((n_zone - 1,)),
            ],
            compiler_params=pltpu.CompilerParams(collective_id=0, has_side_effects=True),
        )(source_field, remap_weights, block_columns, piece_sizes, taps)

    return jax.shard_map(
        shards,
        mesh=mesh,
        in_specs=(
            P("tm", "zone"),
            P("zone", None, None, None),
            P("zone", None),
            P("zone", None),
            P(),
        ),
        out_specs=P("tm", "zone"),
        check_vma=False,
    )
```

```python
import functools

import jax
import jax.numpy as jnp
from jax import lax
from jax.experimental import pallas as pl
from jax.experimental.pallas import tpu as pltpu
from jax.sharding import PartitionSpec as P

MESH = pl.DeviceIdType.MESH
F32 = jnp.float32
BF16 = jnp.bfloat16
SNAP = 8
LANE = 128
BLOCKS = 16
SLOTS = 8
ROWS = 4


def iota(shape, dim):
    return lax.broadcasted_iota(jnp.int32, shape, dim)


def two_parts(value):
    high = value.astype(BF16)
    low = (value - high.astype(F32)).astype(BF16)
    return high, low


def ring_distance(offset, length):
    return min(offset, length - offset)


def plane_offsets(rings, ring, cores):
    span = ring * cores
    offsets = [(dz, dq) for dz in range(rings) for dq in range(span)]
    offsets.remove((0, 0))

    def hops(offset):
        dz, dq = offset
        return ring_distance(dz, rings) + ring_distance(dq // cores, ring)

    return sorted(offsets, key=lambda offset: -hops(offset))


def kernel(
    n_tm,
    n_zone,
    source,
    weights,
    columns,
    sizes,
    taps,
    out,
    x_in,
    x_all,
    w_all,
    cols,
    size_in,
    tap_in,
    toeplitz,
    members,
    send_a,
    recv_a,
    send_b,
    recv_b,
    contrib,
    part_out,
    part_in,
    part_own,
    arranged,
    load_sem,
    x_send,
    x_recv,
    a_send,
    a_recv,
    b_send,
    b_recv,
    p_send,
    p_recv,
    word,
):
    tm = lax.axis_index("tm")
    zone = lax.axis_index("zone")
    rings, ring, cores = 8, 8, 2
    span = ring * cores
    tz, tq = tm // span, lax.rem(tm, span)
    others = []
    for dz, dq in plane_offsets(rings, ring, cores):
        others.append(lax.rem(tz + dz, rings) * span + lax.rem(tq + dq, span))
    zones = [lax.rem(zone + step, n_zone) for step in (2, 1, 3)]

    near, far_y, rows_near, far_z = [], [], [], []
    for step in (2, 6, 1, 7):
        side = lax.rem(tq + step * cores, span)
        near += [tz * span + side, tz * span + side + 1 - 2 * lax.rem(side, cores)]
        rows_near.append(lax.rem(tz + step, rings) * span + tq)
        if step in (2, 6):
            far_y.append(tz * span + side)
            far_z.append(rows_near[-1])
    near.append(tm + 1 - 2 * lax.rem(tm, cores))

    def greet(semaphore, peers):
        for peer in peers:
            pl.semaphore_signal(semaphore, inc=1, device_id={"tm": peer}, device_id_type=MESH)

    barrier = pltpu.get_barrier_semaphore()
    for peer in zones:
        pl.semaphore_signal(barrier, inc=1, device_id={"zone": peer}, device_id_type=MESH)
    greet(barrier, near + rows_near)

    load_x = pltpu.make_async_copy(source, x_in, load_sem.at[0])
    load_c = pltpu.make_async_copy(columns, cols, load_sem.at[1])
    load_w = pltpu.make_async_copy(weights, w_all, load_sem.at[2])
    load_s = pltpu.make_async_copy(sizes, size_in, load_sem.at[3])
    load_t = pltpu.make_async_copy(taps, tap_in, load_sem.at[4])
    for load in (load_x, load_c, load_s, load_w, load_t):
        load.start()

    load_x.wait()
    for i in range(BLOCKS):
        x_all[zone * BLOCKS + i] = x_in[:, i * LANE : (i + 1) * LANE].astype(BF16)
    pl.semaphore_wait(barrier, n_zone - 1 + len(near) + len(rows_near))
    mine = x_all.at[pl.ds(zone * BLOCKS, BLOCKS)]
    x_copies = []
    for n, peer in enumerate(zones):
        x_copies.append(
            pltpu.make_async_remote_copy(
                src_ref=mine,
                dst_ref=mine,
                send_sem=x_send.at[n],
                recv_sem=x_recv.at[n],
                device_id={"zone": peer},
                device_id_type=MESH,
            )
        )
        x_copies[-1].start()
    greet(word.at[0], far_y)

    load_s.wait()
    size_row = size_in[...].astype(F32)
    size_wide = jnp.broadcast_to(size_row, (LANE, LANE))
    upto = jnp.sum(
        jnp.where(iota((LANE, LANE), 1) <= iota((LANE, LANE), 0), size_wide, 0.0), axis=1, keepdims=True
    )
    before = jnp.sum(
        jnp.where(iota((LANE, LANE), 1) < iota((LANE, LANE), 0), size_wide, 0.0), axis=1, keepdims=True
    )
    for i in range(BLOCKS):
        cell = (iota((LANE, LANE), 1) + i * LANE).astype(F32)
        inside = (cell >= before) & (cell < upto)
        members[:, i * LANE : (i + 1) * LANE] = inside.astype(BF16)

    pl.semaphore_wait(word.at[0], len(far_y))
    greet(word.at[1], rows_near)
    load_c.wait()
    load_w.wait()
    pl.semaphore_wait(word.at[1], len(rows_near))
    greet(word.at[2], far_z)
    for copy in x_copies:
        copy.wait_recv()

    stress = []
    for i in range(BLOCKS):
        wind = jnp.zeros((SNAP, LANE), F32)
        for k in range(0, SLOTS, 2):
            x_pair = jnp.concatenate([x_all[cols[k, i]], x_all[cols[k + 1, i]]], axis=1)
            w_pair = jnp.concatenate([w_all[i, k], w_all[i, k + 1]], axis=1)
            wind += lax.dot_general(
                x_pair, w_pair, (((1,), (1,)), ((), ())), preferred_element_type=F32
            )
        stress.append(wind * jnp.abs(wind))

    wide = jnp.concatenate(stress, axis=1)
    high, low = two_parts(wide)
    member = members[...]
    both = jnp.concatenate([high, low], axis=0)
    totals = lax.dot_general(both, member, (((1,), (1,)), ((), ())), preferred_element_type=F32)
    means = (totals[:SNAP] + totals[SNAP:]) / size_row
    high, low = two_parts(means)
    both = jnp.concatenate([high, low], axis=0)
    spread = jnp.dot(both, member, preferred_element_type=F32)
    anomaly = wide - spread[:SNAP] - spread[SNAP:]
    tiles = jnp.concatenate([anomaly[:, i * LANE : (i + 1) * LANE] for i in range(BLOCKS)], axis=0)

    def exchange(send, recv, send_sem, recv_sem):
        for peer in others:
            pltpu.make_async_remote_copy(
                src_ref=send.at[pl.ds(peer, 1)],
                dst_ref=recv.at[pl.ds(tm, 1)],
                send_sem=send_sem,
                recv_sem=recv_sem,
                device_id={"tm": peer},
                device_id_type=MESH,
            ).start()
        recv[pl.ds(tm, 1)] = send[pl.ds(tm, 1)]

    def rows_wait(ref, sem):
        rows = ref.at[pl.ds(0, n_tm - 1)]
        pltpu.make_async_copy(rows, rows, sem).wait()

    send_a[...] = tiles.T.reshape(n_tm, 1, LANE)
    pl.semaphore_wait(word.at[2], len(far_z))
    exchange(send_a, recv_a, a_send, a_recv)

    load_t.wait()
    pieces = []
    for q in range(8):
        row = tap_in[pl.ds(q * LANE - q // 7, LANE)].reshape(1, LANE)
        if q == 7:
            row = jnp.where(iota((1, LANE), 1) < LANE - 1, pltpu.roll(row, LANE - 1, 1), 0.0)
        row = jnp.broadcast_to(row, (8, LANE))
        pieces.append(jnp.where(lax.rem(iota((8, LANE), 1), 8) == iota((8, LANE), 0), row, 0.0))
    spread = jnp.concatenate(pieces, axis=1)
    pick = (iota((1024, LANE), 0) // 8 == iota((1024, LANE), 1)).astype(BF16)
    top, rest = two_parts(spread)
    last = (spread - top.astype(F32) - rest.astype(F32)).astype(BF16)
    by_phase = (
        jnp.dot(top, pick, preferred_element_type=F32)
        + jnp.dot(rest, pick, preferred_element_type=F32)
        + jnp.dot(last, pick, preferred_element_type=F32)
    )
    for n in range(15):
        phase, shift = (n, 63) if n < 8 else (n - 8, 64)
        line = jnp.concatenate([by_phase[phase : phase + 1, :], jnp.zeros((1, LANE), F32)], axis=1)
        turned = pltpu.roll(
            jnp.broadcast_to(line, (LANE, 2 * LANE)), 256 - shift, 1, stride=1, stride_axis=0
        )[:, :LANE]
        high, low = two_parts(turned)
        toeplitz[n * LANE : (n + 1) * LANE, :LANE] = high
        toeplitz[n * LANE : (n + 1) * LANE, LANE:] = low
    rows_wait(recv_a, a_recv)

    series = recv_a[...].reshape(n_tm, LANE)
    high, low = two_parts(series)
    upper = jnp.concatenate([high, low], axis=1)
    lower = jnp.concatenate([high, jnp.zeros_like(high)], axis=1)
    right = jnp.concatenate([upper, lower], axis=0)
    phase = lax.rem(iota((n_tm, LANE), 1), 8)
    filtered = jnp.zeros((n_tm, LANE), F32)
    for n in range(15):
        k = n - 7
        product = jnp.dot(toeplitz[n * LANE : (n + 1) * LANE, :], right, preferred_element_type=F32)
        product = product[:, :LANE] + product[:, LANE:]
        moved = product if k == 0 else pltpu.roll(product, (-k) % LANE, 1)
        filtered += jnp.where((phase + k >= 0) & (phase + k < 8), moved, 0.0)
    send_b[...] = filtered.reshape(n_tm, 1, LANE)
    exchange(send_b, recv_b, b_send, b_recv)

    n_pairs = BLOCKS * SLOTS
    all_blocks = BLOCKS * n_zone
    column_row = jnp.zeros((1, LANE), jnp.int32)
    lane = iota((1, LANE), 1)
    for i in range(BLOCKS):
        for k in range(SLOTS):
            column_row = jnp.where(lane == i * SLOTS + k, cols[k, i], column_row)
    chosen = (iota((all_blocks, LANE), 0) == column_row).astype(BF16)
    chosen = jnp.concatenate([chosen, chosen], axis=1)
    rows_wait(recv_b, b_recv)

    flow = recv_b[...].reshape(n_tm, LANE).T.astype(BF16)
    for i in range(BLOCKS):
        left = flow[i * SNAP : (i + 1) * SNAP, :]
        for k in range(0, SLOTS, 2):
            w_pair = jnp.concatenate([w_all[i, k], w_all[i, k + 1]], axis=1)
            pair = jnp.dot(left, w_pair, preferred_element_type=F32)
            base = (i * SLOTS + k) * SNAP
            contrib[base : base + SNAP, :] = pair[:, :LANE]
            contrib[base + SNAP : base + 2 * SNAP, :] = pair[:, LANE:]
    sums = []
    for t in range(0, SNAP, 2):
        sides = []
        for side in (t, t + 1):
            high, low = two_parts(contrib[pl.ds(side, n_pairs, stride=SNAP), :])
            sides.append(jnp.concatenate([high, low], axis=0))
        both = jnp.dot(chosen, jnp.concatenate(sides, axis=1), preferred_element_type=F32)
        sums += [both[:, :LANE], both[:, LANE:]]
    for t in range(SNAP):
        for z in range(n_zone):
            part = sums[t][z * BLOCKS : (z + 1) * BLOCKS]
            part_out[z, t] = part.astype(BF16)
            part_own[z, t] = part
    p_copies = []
    for n, peer in enumerate(zones):
        p_copies.append(
            pltpu.make_async_remote_copy(
                src_ref=part_out.at[peer],
                dst_ref=part_in.at[n],
                send_sem=p_send.at[n],
                recv_sem=p_recv.at[n],
                device_id={"zone": peer},
                device_id_type=MESH,
            )
        )
        p_copies[-1].start()
    for copy in x_copies:
        copy.wait_send()
    rows_wait(send_a, a_send)
    rows_wait(send_b, b_send)
    for copy in p_copies:
        copy.wait_recv()
    for t in range(SNAP):
        total = part_own[zone, t]
        for n in range(n_zone - 1):
            total += part_in[n, t].astype(F32)
        arranged[pl.ds(t, BLOCKS, stride=SNAP), :] = total
    for i in range(BLOCKS):
        out[:, i * LANE : (i + 1) * LANE] = arranged[i * SNAP : (i + 1) * SNAP, :]
    for copy in p_copies:
        copy.wait_send()


def solution(mesh):
    n_tm, n_zone = mesh.shape["tm"], mesh.shape["zone"]

    def shards(source_field, remap_weights, block_columns, piece_sizes, filter_taps):
        hbm = pl.BlockSpec(memory_space=pltpu.HBM)
        vmem = pl.BlockSpec(memory_space=pltpu.VMEM)
        dma = pltpu.SemaphoreType.DMA
        return pl.pallas_call(
            functools.partial(kernel, n_tm, n_zone),
            name="flux",
            out_shape=jax.ShapeDtypeStruct(source_field.shape, F32),
            in_specs=[hbm] * 5,
            out_specs=vmem,
            scratch_shapes=[
                pltpu.VMEM(source_field.shape, F32),
                pltpu.VMEM((BLOCKS * n_zone, SNAP, LANE), BF16),
                pltpu.VMEM(remap_weights.shape, BF16),
                pltpu.SMEM((SLOTS, BLOCKS), jnp.int32),
                pltpu.VMEM(piece_sizes.shape, jnp.int32),
                pltpu.VMEM(filter_taps.shape, F32),
                pltpu.VMEM((15 * LANE, 2 * LANE), BF16),
                pltpu.VMEM((LANE, BLOCKS * LANE), BF16),
                pltpu.VMEM((n_tm, 1, LANE), F32),
                pltpu.VMEM((n_tm, 1, LANE), F32),
                pltpu.VMEM((n_tm, 1, LANE), F32),
                pltpu.VMEM((n_tm, 1, LANE), F32),
                pltpu.VMEM((BLOCKS * SLOTS * SNAP, LANE), F32),
                pltpu.VMEM((n_zone, SNAP, BLOCKS, LANE), BF16),
                pltpu.VMEM((n_zone - 1, SNAP, BLOCKS, LANE), BF16),
                pltpu.VMEM((n_zone, SNAP, BLOCKS, LANE), F32),
                pltpu.VMEM((BLOCKS * SNAP, LANE), F32),
                dma((5,)),
                dma((n_zone - 1,)),
                dma((n_zone - 1,)),
                dma,
                dma,
                dma,
                dma,
                dma((n_zone - 1,)),
                dma((n_zone - 1,)),
                pltpu.SemaphoreType.REGULAR((3,)),
            ],
            compiler_params=pltpu.CompilerParams(collective_id=0, has_side_effects=True),
        )(source_field, remap_weights, block_columns.T, piece_sizes, filter_taps)

    return jax.shard_map(
        shards,
        mesh=mesh,
        in_specs=(
            P("tm", "zone"),
            P("zone", None, None, None),
            P("zone", None),
            P("zone", None),
            P(),
        ),
        out_specs=P("tm", "zone"),
        check_vma=False,
    )
```

```python
import functools

import jax
import jax.numpy as jnp
from jax import lax
from jax.experimental import pallas as pl
from jax.experimental.pallas import tpu as pltpu
from jax.sharding import PartitionSpec as P

MESH = pl.DeviceIdType.MESH
F32 = jnp.float32
BF16 = jnp.bfloat16
SNAP = 8
LANE = 128
BLOCKS = 16
SLOTS = 8
BANDS = [(0, 0), (0, 1)] + [(g, u) for g in (1, 2, 3) for u in (0, 1, 2)]


def iota(shape, dim):
    return lax.broadcasted_iota(jnp.int32, shape, dim)


def two_parts(value):
    high = value.astype(BF16)
    low = (value - high.astype(F32)).astype(BF16)
    return high, low


def ring_distance(offset, length):
    return min(offset, length - offset)


def kernel(
    n_tm,
    n_zone,
    source,
    weights,
    columns,
    sizes,
    taps,
    out,
    x_in,
    x_all,
    w_all,
    cols,
    size_in,
    tap_in,
    toeplitz,
    members,
    send_a,
    recv_a,
    send_b,
    recv_b,
    contrib,
    part_out,
    part_in,
    part_own,
    arranged,
    load_sem,
    x_send,
    x_recv,
    a_send,
    a_recv,
    b_send,
    b_recv,
    p_send,
    p_recv,
):
    tm = lax.axis_index("tm")
    zone = lax.axis_index("zone")
    rings, ring, cores = 8, 8, 2
    span = ring * cores
    owners = n_tm // 2
    tz, tq = tm // span, lax.rem(tm, span)
    owner = tm < owners
    sides = sorted(range(span), key=lambda dq: -ring_distance(dq // cores, ring))
    zones = [lax.rem(zone + step, n_zone) for step in (2, 1, 3)]

    barrier = pltpu.get_barrier_semaphore()
    for peer in zones:
        pl.semaphore_signal(barrier, inc=1, device_id={"zone": peer}, device_id_type=MESH)

    @pl.when(owner)
    def _():
        @pl.loop(1, n_tm)
        def _(step):
            peer = lax.rem(tm + step, n_tm)
            pl.semaphore_signal(barrier, inc=1, device_id={"tm": peer}, device_id_type=MESH)

    load_x = pltpu.make_async_copy(source, x_in, load_sem.at[0])
    load_c = pltpu.make_async_copy(columns, cols, load_sem.at[1])
    load_w = pltpu.make_async_copy(weights, w_all, load_sem.at[2])
    load_s = pltpu.make_async_copy(sizes, size_in, load_sem.at[3])
    load_t = pltpu.make_async_copy(taps, tap_in, load_sem.at[4])
    for load in (load_x, load_c, load_s, load_w, load_t):
        load.start()

    load_x.wait()
    for i in range(BLOCKS):
        x_all[zone * BLOCKS + i] = x_in[:, i * LANE : (i + 1) * LANE].astype(BF16)
    pl.semaphore_wait(barrier, n_zone - 1 + owners - owner.astype(jnp.int32))
    mine = x_all.at[pl.ds(zone * BLOCKS, BLOCKS)]
    x_copies = []
    for n, peer in enumerate(zones):
        x_copies.append(
            pltpu.make_async_remote_copy(
                src_ref=mine,
                dst_ref=mine,
                send_sem=x_send.at[n],
                recv_sem=x_recv.at[n],
                device_id={"zone": peer},
                device_id_type=MESH,
            )
        )
        x_copies[-1].start()

    load_s.wait()
    size_row = size_in[...].astype(F32)
    size_wide = jnp.broadcast_to(size_row, (LANE, LANE))
    upto = jnp.sum(
        jnp.where(iota((LANE, LANE), 1) <= iota((LANE, LANE), 0), size_wide, 0.0), axis=1, keepdims=True
    )
    before = jnp.sum(
        jnp.where(iota((LANE, LANE), 1) < iota((LANE, LANE), 0), size_wide, 0.0), axis=1, keepdims=True
    )
    for i in range(BLOCKS):
        cell = (iota((LANE, LANE), 1) + i * LANE).astype(F32)
        inside = (cell >= before) & (cell < upto)
        members[:, i * LANE : (i + 1) * LANE] = inside.astype(BF16)

    load_t.wait()
    load_c.wait()
    load_w.wait()
    for copy in x_copies:
        copy.wait_recv()

    stress = []
    for i in range(BLOCKS):
        wind = jnp.zeros((SNAP, LANE), F32)
        for k in range(0, SLOTS, 2):
            x_pair = jnp.concatenate([x_all[cols[k, i]], x_all[cols[k + 1, i]]], axis=1)
            w_pair = jnp.concatenate([w_all[i, k], w_all[i, k + 1]], axis=1)
            wind += lax.dot_general(
                x_pair, w_pair, (((1,), (1,)), ((), ())), preferred_element_type=F32
            )
        stress.append(wind * jnp.abs(wind))

    wide = jnp.concatenate(stress, axis=1)
    high, low = two_parts(wide)
    member = members[...]
    both = jnp.concatenate([high, low], axis=0)
    totals = lax.dot_general(both, member, (((1,), (1,)), ((), ())), preferred_element_type=F32)
    means = (totals[:SNAP] + totals[SNAP:]) / size_row
    high, low = two_parts(means)
    both = jnp.concatenate([high, low], axis=0)
    spread = jnp.dot(both, member, preferred_element_type=F32)
    anomaly = wide - spread[:SNAP] - spread[SNAP:]
    tiles = jnp.concatenate([anomaly[:, i * LANE : (i + 1) * LANE] for i in range(BLOCKS)], axis=0)

    def rows_wait(ref, rows, sem):
        part = ref.at[pl.ds(0, rows)]
        pltpu.make_async_copy(part, part, sem).wait()

    def rows_wait_owners(ref, sem):
        @pl.when(owner)
        def _():
            rows_wait(ref, 2 * owners - 2, sem)

        @pl.when(jnp.logical_not(owner))
        def _():
            rows_wait(ref, 2 * owners, sem)

    turned = tiles.T
    first, second = turned[:owners], turned[owners:]
    odd = lax.rem(iota((owners, LANE), 1) // 4, 2) == 1
    send_a[pl.ds(0, owners, stride=2)] = jnp.where(odd, pltpu.roll(second, 4, 1), first).reshape(
        owners, 1, LANE
    )
    send_a[pl.ds(1, owners, stride=2)] = jnp.where(odd, second, pltpu.roll(first, LANE - 4, 1)).reshape(
        owners, 1, LANE
    )

    def send_row(peer):
        pltpu.make_async_remote_copy(
            src_ref=send_a.at[pl.ds(2 * peer, 2)],
            dst_ref=recv_a.at[pl.ds(2 * tm, 2)],
            send_sem=a_send,
            recv_sem=a_recv,
            device_id={"tm": peer},
            device_id_type=MESH,
        ).start()

    steps = [(j, dq) for j in range(4) for dq in range(span)]
    steps.sort(key=lambda step: -((4, 3, 2, 3)[step[0]] + ring_distance(step[1] // cores, ring)))
    for j, dq in steps:
        peer = lax.rem(tz + j, 4) * span + lax.rem(tq + dq, span)
        if j == 0 and dq == 0:
            pl.when(jnp.logical_not(owner))(functools.partial(send_row, peer))
        else:
            send_row(peer)

    @pl.when(owner)
    def _():
        recv_a[pl.ds(2 * tm, 2)] = send_a[pl.ds(2 * tm, 2)]

        pieces = []
        for q in range(8):
            row = tap_in[pl.ds(q * LANE - q // 7, LANE)].reshape(1, LANE)
            if q == 7:
                row = jnp.where(iota((1, LANE), 1) < LANE - 1, pltpu.roll(row, LANE - 1, 1), 0.0)
            row = jnp.broadcast_to(row, (8, LANE))
            pieces.append(jnp.where(lax.rem(iota((8, LANE), 1), 4) == iota((8, LANE), 0), row, 0.0))
        spread = jnp.concatenate(pieces, axis=1)
        pick = (iota((1024, 256), 0) // 4 == iota((1024, 256), 1)).astype(BF16)
        top, rest = two_parts(spread)
        last = (spread - top.astype(F32) - rest.astype(F32)).astype(BF16)
        by_phase = (
            jnp.dot(top, pick, preferred_element_type=F32)
            + jnp.dot(rest, pick, preferred_element_type=F32)
            + jnp.dot(last, pick, preferred_element_type=F32)
        )
        for n, (g, u) in enumerate(BANDS):
            phase, start = (3, 127) if g == 0 else (g - 1, 128)
            line = jnp.concatenate([by_phase[phase : phase + 1, :], jnp.zeros((1, 256), F32)], axis=1)
            wide = jnp.broadcast_to(line, (LANE, 512))
            high, low = two_parts(pltpu.roll(wide, (u - start) % 512, 1, stride=2, stride_axis=0)[:, :256])
            for z in range(rings):
                toeplitz[z, n * span : (n + 1) * span, :256] = high[z * span : (z + 1) * span]
                toeplitz[z, n * span : (n + 1) * span, 256:] = low[z * span : (z + 1) * span]
        rows_wait(recv_a, 2 * n_tm - 2, a_recv)

        high, low = two_parts(recv_a[...].reshape(2 * n_tm, LANE))
        upper = jnp.concatenate([high, low], axis=1)
        lower = jnp.concatenate([high, jnp.zeros_like(high)], axis=1)
        right = jnp.concatenate([upper, lower], axis=0)
        place = lax.rem(iota((span, LANE), 1), 4)
        for z in range(rings):
            product = jnp.dot(toeplitz[z], right, preferred_element_type=F32)
            product = product[:, :LANE] + product[:, LANE:]
            band = {b: product[n * span : (n + 1) * span] for n, b in enumerate(BANDS)}
            for u in range(2):
                total = band[0, u]
                for g in (1, 2, 3):
                    total += jnp.where(
                        place < 4 - g,
                        pltpu.roll(band[g, u], LANE - g, 1),
                        pltpu.roll(band[g, u + 1], 4 - g, 1),
                    )
                send_b[pl.ds(2 * z * span + u, span, stride=2)] = total.reshape(span, 1, LANE)

            def send_back(peer):
                pltpu.make_async_remote_copy(
                    src_ref=send_b.at[pl.ds(2 * peer, 2)],
                    dst_ref=recv_b.at[pl.ds(2 * tm, 2)],
                    send_sem=b_send,
                    recv_sem=b_recv,
                    device_id={"tm": peer},
                    device_id_type=MESH,
                ).start()

            for dq in sides:
                peer = z * span + lax.rem(tq + dq, span)
                if z < rings // 2 and dq == 0:
                    pl.when(tz != z)(functools.partial(send_back, peer))
                else:
                    send_back(peer)
        recv_b[pl.ds(2 * tm, 2)] = send_b[pl.ds(2 * tm, 2)]

    n_pairs = BLOCKS * SLOTS
    all_blocks = BLOCKS * n_zone
    column_row = jnp.zeros((1, LANE), jnp.int32)
    lane = iota((1, LANE), 1)
    for i in range(BLOCKS):
        for k in range(SLOTS):
            column_row = jnp.where(lane == i * SLOTS + k, cols[k, i], column_row)
    chosen = (iota((all_blocks, LANE), 0) == column_row).astype(BF16)
    chosen = jnp.concatenate([chosen, chosen], axis=1)
    rows_wait_owners(recv_b, b_recv)

    even_row = recv_b[pl.ds(0, owners, stride=2)].reshape(owners, LANE)
    odd_row = recv_b[pl.ds(1, owners, stride=2)].reshape(owners, LANE)
    first = jnp.where(odd, pltpu.roll(odd_row, 4, 1), even_row)
    second = jnp.where(odd, odd_row, pltpu.roll(even_row, LANE - 4, 1))
    flow = jnp.concatenate([first, second], axis=0).T.astype(BF16)
    for i in range(BLOCKS):
        left = flow[i * SNAP : (i + 1) * SNAP, :]
        for k in range(0, SLOTS, 2):
            w_pair = jnp.concatenate([w_all[i, k], w_all[i, k + 1]], axis=1)
            pair = jnp.dot(left, w_pair, preferred_element_type=F32)
            base = (i * SLOTS + k) * SNAP
            contrib[base : base + SNAP, :] = pair[:, :LANE]
            contrib[base + SNAP : base + 2 * SNAP, :] = pair[:, LANE:]
    sums = []
    for t in range(0, SNAP, 2):
        sides = []
        for side in (t, t + 1):
            high, low = two_parts(contrib[pl.ds(side, n_pairs, stride=SNAP), :])
            sides.append(jnp.concatenate([high, low], axis=0))
        both = jnp.dot(chosen, jnp.concatenate(sides, axis=1), preferred_element_type=F32)
        sums += [both[:, :LANE], both[:, LANE:]]
    for t in range(SNAP):
        for z in range(n_zone):
            part = sums[t][z * BLOCKS : (z + 1) * BLOCKS]
            part_out[z, t] = part.astype(BF16)
            part_own[z, t] = part
    p_copies = []
    for n, peer in enumerate(zones):
        p_copies.append(
            pltpu.make_async_remote_copy(
                src_ref=part_out.at[peer],
                dst_ref=part_in.at[n],
                send_sem=p_send.at[n],
                recv_sem=p_recv.at[n],
                device_id={"zone": peer},
                device_id_type=MESH,
            )
        )
        p_copies[-1].start()
    for copy in x_copies:
        copy.wait_send()
    rows_wait_owners(send_a, a_send)

    @pl.when(owner)
    def _():
        rows_wait(send_b, 2 * n_tm - 2, b_send)

    for copy in p_copies:
        copy.wait_recv()
    for t in range(SNAP):
        total = part_own[zone, t]
        for n in range(n_zone - 1):
            total += part_in[n, t].astype(F32)
        arranged[pl.ds(t, BLOCKS, stride=SNAP), :] = total
    for i in range(BLOCKS):
        out[:, i * LANE : (i + 1) * LANE] = arranged[i * SNAP : (i + 1) * SNAP, :]
    for copy in p_copies:
        copy.wait_send()


def solution(mesh):
    n_tm, n_zone = mesh.shape["tm"], mesh.shape["zone"]

    def shards(source_field, remap_weights, block_columns, piece_sizes, filter_taps):
        hbm = pl.BlockSpec(memory_space=pltpu.HBM)
        vmem = pl.BlockSpec(memory_space=pltpu.VMEM)
        dma = pltpu.SemaphoreType.DMA
        return pl.pallas_call(
            functools.partial(kernel, n_tm, n_zone),
            name="flux",
            out_shape=pltpu.VMEM(source_field.shape, F32),
            in_specs=[hbm] * 5,
            out_specs=vmem,
            scratch_shapes=[
                pltpu.VMEM(source_field.shape, F32),
                pltpu.VMEM((BLOCKS * n_zone, SNAP, LANE), BF16),
                pltpu.VMEM(remap_weights.shape, BF16),
                pltpu.SMEM((SLOTS, BLOCKS), jnp.int32),
                pltpu.VMEM(piece_sizes.shape, jnp.int32),
                pltpu.VMEM(filter_taps.shape, F32),
                pltpu.VMEM((8, len(BANDS) * 16, 512), BF16),
                pltpu.VMEM((LANE, BLOCKS * LANE), BF16),
                pltpu.VMEM((n_tm, 1, LANE), F32),
                pltpu.VMEM((2 * n_tm, 1, LANE), F32),
                pltpu.VMEM((2 * n_tm, 1, LANE), F32),
                pltpu.VMEM((n_tm, 1, LANE), F32),
                pltpu.VMEM((BLOCKS * SLOTS * SNAP, LANE), F32),
                pltpu.VMEM((n_zone, SNAP, BLOCKS, LANE), BF16),
                pltpu.VMEM((n_zone - 1, SNAP, BLOCKS, LANE), BF16),
                pltpu.VMEM((n_zone, SNAP, BLOCKS, LANE), F32),
                pltpu.VMEM((BLOCKS * SNAP, LANE), F32),
                dma((5,)),
                dma((n_zone - 1,)),
                dma((n_zone - 1,)),
                dma,
                dma,
                dma,
                dma,
                dma((n_zone - 1,)),
                dma((n_zone - 1,)),
            ],
            compiler_params=pltpu.CompilerParams(collective_id=0, has_side_effects=True),
        )(source_field, remap_weights, block_columns.T, piece_sizes, filter_taps)

    return jax.shard_map(
        shards,
        mesh=mesh,
        in_specs=(
            P("tm", "zone"),
            P("zone", None, None, None),
            P("zone", None),
            P("zone", None),
            P(),
        ),
        out_specs=P("tm", "zone"),
        check_vma=False,
    )
```

```python
import functools

import jax
import jax.numpy as jnp
from jax import lax
from jax.experimental import pallas as pl
from jax.experimental.pallas import tpu as pltpu
from jax.sharding import PartitionSpec as P

MESH = pl.DeviceIdType.MESH
F32 = jnp.float32
BF16 = jnp.bfloat16
SNAP = 8
LANE = 128
BLOCKS = 16
SLOTS = 8
SLABS = [(0, 1), (2, 3), (4, 5, 6, 7)]
BANDS = [(0, 0), (0, 1)] + [(g, u) for g in (1, 2, 3) for u in (0, 1, 2)]


def iota(shape, dim):
    return lax.broadcasted_iota(jnp.int32, shape, dim)


def two_parts(value):
    high = value.astype(BF16)
    low = (value - high.astype(F32)).astype(BF16)
    return high, low


def ring_distance(offset, length):
    return min(offset, length - offset)


def kernel(
    n_tm,
    n_zone,
    source,
    weights,
    columns,
    sizes,
    taps,
    out,
    x_in,
    x_all,
    w_all,
    w_turned,
    cols,
    size_in,
    tap_in,
    toeplitz,
    members,
    members_tall,
    send_a,
    recv_a,
    send_b,
    recv_b,
    contrib,
    part_out,
    part_in,
    part_own,
    arranged,
    load_sem,
    x_send,
    x_recv,
    a_send,
    a_recv,
    b_send,
    b_recv,
    p_send,
    p_recv,
    word,
):
    tm = lax.axis_index("tm")
    zone = lax.axis_index("zone")
    rings, ring, cores = 8, 8, 2
    span = ring * cores
    owners = n_tm // 2
    tz, tq = tm // span, lax.rem(tm, span)
    owner = tm < owners
    sides = sorted(range(span), key=lambda dq: -ring_distance(dq // cores, ring))
    zones = [lax.rem(zone + step, n_zone) for step in (2, 1, 3)]

    core = lax.rem(tq, cores)

    def beside(step):
        return tz * span + lax.rem(tq + step * cores + span, span)

    def greet(semaphore, peer):
        pl.semaphore_signal(semaphore, inc=1, device_id={"tm": peer}, device_id_type=MESH)

    barrier = pltpu.get_barrier_semaphore()
    for peer in zones:
        pl.semaphore_signal(barrier, inc=1, device_id={"zone": peer}, device_id_type=MESH)
    lines = [lax.rem(tz + dz, 4) * span + tq for dz in (1, 2, 3)]
    host = jnp.where(tz < 6, 3, 0) * span + tq
    hosting = (tz == 0) | (tz == 3)
    guests = [jnp.where(tz == 0, far, near) * span + tq for far, near in ((7, 4), (6, 5))]

    @pl.when(owner)
    def _():
        for step in (2, -2, 1, -1):
            greet(barrier, beside(step))
            greet(barrier, beside(step) + 1 - 2 * core)
        greet(barrier, tm + 1 - 2 * core)
        for peer in lines:
            greet(barrier, peer)

    @pl.when(hosting)
    def _():
        for peer in guests:
            greet(barrier, peer)

    load_x = pltpu.make_async_copy(source, x_in, load_sem.at[0])
    load_c = pltpu.make_async_copy(columns, cols, load_sem.at[1])
    load_w = pltpu.make_async_copy(weights, w_all, load_sem.at[2])
    load_s = pltpu.make_async_copy(sizes, size_in, load_sem.at[3])
    load_t = pltpu.make_async_copy(taps, tap_in, load_sem.at[4])
    for load in (load_x, load_c, load_s, load_w, load_t):
        load.start()

    load_x.wait()
    for i in range(BLOCKS):
        x_all[zone * BLOCKS + i] = x_in[:, i * LANE : (i + 1) * LANE].astype(BF16)
    pl.semaphore_wait(barrier, n_zone - 1 + jnp.where(owner, 12, 1))
    mine = x_all.at[pl.ds(zone * BLOCKS, BLOCKS)]
    x_copies = []
    for n, peer in enumerate(zones):
        x_copies.append(
            pltpu.make_async_remote_copy(
                src_ref=mine,
                dst_ref=mine,
                send_sem=x_send.at[n],
                recv_sem=x_recv.at[n],
                device_id={"zone": peer},
                device_id_type=MESH,
            )
        )
        x_copies[-1].start()

    @pl.when(owner)
    def _():
        for step in (2, -2):
            greet(word.at[0], beside(step))

    @pl.when(jnp.logical_not(owner))
    def _():
        greet(word.at[2], host)

    load_s.wait()
    size_row = size_in[...].astype(F32)
    down, along = iota((LANE, LANE), 0), iota((LANE, LANE), 1)
    size_wide = jnp.broadcast_to(size_row, (LANE, LANE))
    size_tall = size_wide.T
    upto = jnp.sum(jnp.where(along <= down, size_wide, 0.0), axis=1, keepdims=True)
    before = jnp.sum(jnp.where(along < down, size_wide, 0.0), axis=1, keepdims=True)
    upto_row = jnp.sum(jnp.where(down <= along, size_tall, 0.0), axis=0, keepdims=True)
    before_row = jnp.sum(jnp.where(down < along, size_tall, 0.0), axis=0, keepdims=True)
    for i in range(BLOCKS):
        cell = (along + i * LANE).astype(F32)
        inside = (cell >= before) & (cell < upto)
        members[:, i * LANE : (i + 1) * LANE] = inside.astype(BF16)
        cell = (down + i * LANE).astype(F32)
        inside = (cell >= before_row) & (cell < upto_row)
        members_tall[i * LANE : (i + 1) * LANE, :] = inside.astype(BF16)

    @pl.when(owner)
    def _():
        pl.semaphore_wait(word.at[0], 2)
        for peer in lines:
            greet(word.at[1], peer)

    load_t.wait()
    load_c.wait()
    load_w.wait()
    for i in range(BLOCKS):
        for k in range(SLOTS):
            w_turned[i, k * LANE : (k + 1) * LANE, :] = w_all[i, k].T
    for copy in x_copies:
        copy.wait_recv()

    stress = []
    for i in range(BLOCKS):
        picked = jnp.concatenate([x_all[cols[k, i]] for k in range(SLOTS)], axis=1)
        wind = jnp.dot(picked, w_turned[i], preferred_element_type=F32)
        stress.append(wind * jnp.abs(wind))

    wide = jnp.concatenate(stress, axis=1)
    high, low = two_parts(wide)
    both = jnp.concatenate([high, low], axis=0)
    totals = jnp.dot(both, members_tall[...], preferred_element_type=F32)
    means = (totals[:SNAP] + totals[SNAP:]) / size_row
    high, low = two_parts(means)
    both = jnp.concatenate([high, low], axis=0)
    spread = jnp.dot(both, members[...], preferred_element_type=F32)
    anomaly = wide - spread[:SNAP] - spread[SNAP:]
    tiles = jnp.concatenate([anomaly[:, i * LANE : (i + 1) * LANE] for i in range(BLOCKS)], axis=0)

    def rows_wait(ref, rows, sem):
        part = ref.at[pl.ds(0, rows)]
        pltpu.make_async_copy(part, part, sem).wait()

    def rows_wait_owners(ref, sem):
        @pl.when(owner)
        def _():
            rows_wait(ref, 2 * owners - 2, sem)

        @pl.when(jnp.logical_not(owner))
        def _():
            rows_wait(ref, 2 * owners, sem)

    turned = tiles.T
    first, second = turned[:owners], turned[owners:]
    odd = lax.rem(iota((owners, LANE), 1) // 4, 2) == 1
    send_a[pl.ds(0, owners, stride=2)] = jnp.where(odd, pltpu.roll(second, 4, 1), first).reshape(
        owners, 1, LANE
    )
    send_a[pl.ds(1, owners, stride=2)] = jnp.where(odd, second, pltpu.roll(first, LANE - 4, 1)).reshape(
        owners, 1, LANE
    )

    def send_row(peer):
        pltpu.make_async_remote_copy(
            src_ref=send_a.at[pl.ds(2 * peer, 2)],
            dst_ref=recv_a.at[pl.ds(2 * tm, 2)],
            send_sem=a_send,
            recv_sem=a_recv,
            device_id={"tm": peer},
            device_id_type=MESH,
        ).start()

    steps = [(j, dq) for j in range(4) for dq in range(span)]
    steps.sort(key=lambda step: -((4, 3, 2, 3)[step[0]] + ring_distance(step[1] // cores, ring)))

    @pl.when(owner)
    def _():
        pl.semaphore_wait(word.at[1], 3)

    @pl.when(jnp.logical_not(owner))
    def _():
        pl.semaphore_wait(word.at[3], 1)

    for j, dq in steps:
        peer = lax.rem(tz + j, 4) * span + lax.rem(tq + dq, span)
        if j == 0 and dq == 0:
            pl.when(jnp.logical_not(owner))(functools.partial(send_row, peer))
        else:
            send_row(peer)

    @pl.when(hosting)
    def _():
        pl.semaphore_wait(word.at[2], 2)
        for peer in guests:
            greet(word.at[3], peer)

    @pl.when(owner)
    def _():
        recv_a[pl.ds(2 * tm, 2)] = send_a[pl.ds(2 * tm, 2)]

        pieces = []
        for q in range(8):
            row = tap_in[pl.ds(q * LANE - q // 7, LANE)].reshape(1, LANE)
            if q == 7:
                row = jnp.where(iota((1, LANE), 1) < LANE - 1, pltpu.roll(row, LANE - 1, 1), 0.0)
            row = jnp.broadcast_to(row, (8, LANE))
            pieces.append(jnp.where(lax.rem(iota((8, LANE), 1), 4) == iota((8, LANE), 0), row, 0.0))
        spread = jnp.concatenate(pieces, axis=1)
        pick = (iota((1024, 256), 0) // 4 == iota((1024, 256), 1)).astype(BF16)
        top, rest = two_parts(spread)
        last = (spread - top.astype(F32) - rest.astype(F32)).astype(BF16)
        by_phase = (
            jnp.dot(top, pick, preferred_element_type=F32)
            + jnp.dot(rest, pick, preferred_element_type=F32)
            + jnp.dot(last, pick, preferred_element_type=F32)
        )
        for n, (g, u) in enumerate(BANDS):
            phase, start = (3, 127) if g == 0 else (g - 1, 128)
            line = jnp.concatenate([by_phase[phase : phase + 1, :], jnp.zeros((1, 256), F32)], axis=1)
            wide = jnp.broadcast_to(line, (LANE, 512))
            high, low = two_parts(pltpu.roll(wide, (u - start) % 512, 1, stride=2, stride_axis=0)[:, :256])
            for slab, ref in zip(SLABS, toeplitz):
                rows, base = len(slab) * span, slab[0] * span
                ref[n * rows : (n + 1) * rows, :256] = high[base : base + rows]
                ref[n * rows : (n + 1) * rows, 256:] = low[base : base + rows]
        rows_wait(recv_a, 2 * n_tm - 2, a_recv)

        high, low = two_parts(recv_a[...].reshape(2 * n_tm, LANE))
        upper = jnp.concatenate([high, low], axis=1)
        lower = jnp.concatenate([high, jnp.zeros_like(high)], axis=1)
        right = jnp.concatenate([upper, lower], axis=0)

        def send_back(peer):
            pltpu.make_async_remote_copy(
                src_ref=send_b.at[pl.ds(2 * peer, 2)],
                dst_ref=recv_b.at[pl.ds(2 * tm, 2)],
                send_sem=b_send,
                recv_sem=b_recv,
                device_id={"tm": peer},
                device_id_type=MESH,
            ).start()

        for slab, ref in zip(SLABS, toeplitz):
            rows, base = len(slab) * span, slab[0] * span
            place = lax.rem(iota((rows, LANE), 1), 4)
            product = jnp.dot(ref[...], right, preferred_element_type=F32)
            product = product[:, :LANE] + product[:, LANE:]
            band = {b: product[n * rows : (n + 1) * rows] for n, b in enumerate(BANDS)}
            for u in range(2):
                total = band[0, u]
                for g in (1, 2, 3):
                    total += jnp.where(
                        place < 4 - g,
                        pltpu.roll(band[g, u], LANE - g, 1),
                        pltpu.roll(band[g, u + 1], 4 - g, 1),
                    )
                send_b[pl.ds(2 * base + u, rows, stride=2)] = total.reshape(rows, 1, LANE)
            for z in slab:
                for dq in sides:
                    peer = z * span + lax.rem(tq + dq, span)
                    if z < rings // 2 and dq == 0:
                        pl.when(tz != z)(functools.partial(send_back, peer))
                    else:
                        send_back(peer)
        recv_b[pl.ds(2 * tm, 2)] = send_b[pl.ds(2 * tm, 2)]

    n_pairs = BLOCKS * SLOTS
    all_blocks = BLOCKS * n_zone
    column_row = jnp.zeros((1, LANE), jnp.int32)
    lane = iota((1, LANE), 1)
    for i in range(BLOCKS):
        for k in range(SLOTS):
            column_row = jnp.where(lane == i * SLOTS + k, cols[k, i], column_row)
    chosen = (iota((all_blocks, LANE), 0) == column_row).astype(BF16)
    chosen = jnp.concatenate([chosen, chosen], axis=1)
    rows_wait_owners(recv_b, b_recv)

    even_row = recv_b[pl.ds(0, owners, stride=2)].reshape(owners, LANE)
    odd_row = recv_b[pl.ds(1, owners, stride=2)].reshape(owners, LANE)
    first = jnp.where(odd, pltpu.roll(odd_row, 4, 1), even_row)
    second = jnp.where(odd, odd_row, pltpu.roll(even_row, LANE - 4, 1))
    flow = jnp.concatenate([first, second], axis=0).T.astype(BF16)
    for i in range(BLOCKS):
        left = flow[i * SNAP : (i + 1) * SNAP, :]
        for k in range(0, SLOTS, 2):
            w_pair = jnp.concatenate([w_all[i, k], w_all[i, k + 1]], axis=1)
            pair = jnp.dot(left, w_pair, preferred_element_type=F32)
            base = (i * SLOTS + k) * SNAP
            contrib[base : base + SNAP, :] = pair[:, :LANE]
            contrib[base + SNAP : base + 2 * SNAP, :] = pair[:, LANE:]
    sums = []
    for t in range(0, SNAP, 2):
        sides = []
        for side in (t, t + 1):
            high, low = two_parts(contrib[pl.ds(side, n_pairs, stride=SNAP), :])
            sides.append(jnp.concatenate([high, low], axis=0))
        both = jnp.dot(chosen, jnp.concatenate(sides, axis=1), preferred_element_type=F32)
        sums += [both[:, :LANE], both[:, LANE:]]
    for t in range(SNAP):
        for z in range(n_zone):
            part = sums[t][z * BLOCKS : (z + 1) * BLOCKS]
            part_out[z, t] = part.astype(BF16)
            part_own[z, t] = part
    p_copies = []
    for n, peer in enumerate(zones):
        p_copies.append(
            pltpu.make_async_remote_copy(
                src_ref=part_out.at[peer],
                dst_ref=part_in.at[n],
                send_sem=p_send.at[n],
                recv_sem=p_recv.at[n],
                device_id={"zone": peer},
                device_id_type=MESH,
            )
        )
        p_copies[-1].start()
    for copy in x_copies:
        copy.wait_send()
    rows_wait_owners(send_a, a_send)

    @pl.when(owner)
    def _():
        rows_wait(send_b, 2 * n_tm - 2, b_send)

    for copy in p_copies:
        copy.wait_recv()
    for t in range(SNAP):
        total = part_own[zone, t]
        for n in range(n_zone - 1):
            total += part_in[n, t].astype(F32)
        arranged[pl.ds(t, BLOCKS, stride=SNAP), :] = total
    for i in range(BLOCKS):
        out[:, i * LANE : (i + 1) * LANE] = arranged[i * SNAP : (i + 1) * SNAP, :]
    for copy in p_copies:
        copy.wait_send()


def solution(mesh):
    n_tm, n_zone = mesh.shape["tm"], mesh.shape["zone"]

    def shards(source_field, remap_weights, block_columns, piece_sizes, filter_taps):
        hbm = pl.BlockSpec(memory_space=pltpu.HBM)
        vmem = pl.BlockSpec(memory_space=pltpu.VMEM)
        dma = pltpu.SemaphoreType.DMA
        return pl.pallas_call(
            functools.partial(kernel, n_tm, n_zone),
            name="flux",
            out_shape=pltpu.VMEM(source_field.shape, F32),
            in_specs=[hbm] * 5,
            out_specs=vmem,
            scratch_shapes=[
                pltpu.VMEM(source_field.shape, F32),
                pltpu.VMEM((BLOCKS * n_zone, SNAP, LANE), BF16),
                pltpu.VMEM(remap_weights.shape, BF16),
                pltpu.VMEM((BLOCKS, SLOTS * LANE, LANE), BF16),
                pltpu.SMEM((SLOTS, BLOCKS), jnp.int32),
                pltpu.VMEM(piece_sizes.shape, jnp.int32),
                pltpu.VMEM(filter_taps.shape, F32),
                [pltpu.VMEM((len(BANDS) * len(slab) * 16, 512), BF16) for slab in SLABS],
                pltpu.VMEM((LANE, BLOCKS * LANE), BF16),
                pltpu.VMEM((BLOCKS * LANE, LANE), BF16),
                pltpu.VMEM((n_tm, 1, LANE), F32),
                pltpu.VMEM((2 * n_tm, 1, LANE), F32),
                pltpu.VMEM((2 * n_tm, 1, LANE), F32),
                pltpu.VMEM((n_tm, 1, LANE), F32),
                pltpu.VMEM((BLOCKS * SLOTS * SNAP, LANE), F32),
                pltpu.VMEM((n_zone, SNAP, BLOCKS, LANE), BF16),
                pltpu.VMEM((n_zone - 1, SNAP, BLOCKS, LANE), BF16),
                pltpu.VMEM((n_zone, SNAP, BLOCKS, LANE), F32),
                pltpu.VMEM((BLOCKS * SNAP, LANE), F32),
                dma((5,)),
                dma((n_zone - 1,)),
                dma((n_zone - 1,)),
                dma,
                dma,
                dma,
                dma,
                dma((n_zone - 1,)),
                dma((n_zone - 1,)),
                pltpu.SemaphoreType.REGULAR((4,)),
            ],
            compiler_params=pltpu.CompilerParams(collective_id=0, has_side_effects=True),
        )(source_field, remap_weights, block_columns.T, piece_sizes, filter_taps)

    return jax.shard_map(
        shards,
        mesh=mesh,
        in_specs=(
            P("tm", "zone"),
            P("zone", None, None, None),
            P("zone", None),
            P("zone", None),
            P(),
        ),
        out_specs=P("tm", "zone"),
        check_vma=False,
    )
```

```python
import functools

import jax
import jax.numpy as jnp
from jax import lax
from jax.experimental import pallas as pl
from jax.experimental.pallas import tpu as pltpu
from jax.sharding import PartitionSpec as P

MESH = pl.DeviceIdType.MESH
F32 = jnp.float32
BF16 = jnp.bfloat16
SNAP = 8
LANE = 128
BLOCKS = 16
SLOTS = 8
SLABS = [(0, 1), (2, 3), (4, 5, 6, 7)]
BANDS = [(0, 0), (0, 1)] + [(g, u) for g in (1, 2, 3) for u in (0, 1, 2)]


def iota(shape, dim):
    return lax.broadcasted_iota(jnp.int32, shape, dim)


def two_parts(value):
    high = value.astype(BF16)
    low = (value - high.astype(F32)).astype(BF16)
    return high, low


def ring_distance(offset, length):
    return min(offset, length - offset)


def kernel(
    n_tm,
    n_zone,
    source,
    weights,
    columns,
    sizes,
    taps,
    out,
    x_in,
    x_all,
    w_all,
    w_turned,
    cols,
    size_in,
    tap_in,
    toeplitz,
    members,
    members_tall,
    send_a,
    recv_a,
    send_b,
    recv_b,
    paired,
    contrib,
    part_out,
    part_in,
    part_own,
    arranged,
    load_sem,
    x_send,
    x_recv,
    a_send,
    a_recv,
    b_send,
    b_recv,
    p_send,
    p_recv,
    word,
):
    tm = lax.axis_index("tm")
    zone = lax.axis_index("zone")
    rings, ring, cores = 8, 8, 2
    span = ring * cores
    owners = n_tm // 2
    tz, tq = tm // span, lax.rem(tm, span)
    owner = tm < owners
    sides = sorted(range(span), key=lambda dq: -ring_distance(dq // cores, ring))
    zones = [lax.rem(zone + step, n_zone) for step in (2, 1, 3)]

    core = lax.rem(tq, cores)

    def beside(step):
        return tz * span + lax.rem(tq + step * cores + span, span)

    def greet(semaphore, peer):
        pl.semaphore_signal(semaphore, inc=1, device_id={"tm": peer}, device_id_type=MESH)

    zone_order = [
        jnp.where(zone == 2, 1, 2),
        jnp.where((zone == 1) | (zone == 2), 3, 1),
        jnp.where(zone == 0, 3, 0),
    ]

    barrier = pltpu.get_barrier_semaphore()
    for peer in zones:
        pl.semaphore_signal(barrier, inc=1, device_id={"zone": peer}, device_id_type=MESH)
    lines = [lax.rem(tz + dz, 4) * span + tq for dz in (1, 2, 3)]
    host = jnp.where(tz < 6, 3, 0) * span + tq
    hosting = (tz == 0) | (tz == 3)
    guests = [jnp.where(tz == 0, far, near) * span + tq for far, near in ((7, 4), (6, 5))]

    @pl.when(owner)
    def _():
        for step in (2, -2, 1, -1):
            greet(barrier, beside(step))
            greet(barrier, beside(step) + 1 - 2 * core)
        greet(barrier, tm + 1 - 2 * core)
        for peer in lines:
            greet(barrier, peer)

    @pl.when(hosting)
    def _():
        for peer in guests:
            greet(barrier, peer)

    load_x = pltpu.make_async_copy(source, x_in, load_sem.at[0])
    load_c = pltpu.make_async_copy(columns, cols, load_sem.at[1])
    load_w = pltpu.make_async_copy(weights, w_all, load_sem.at[2])
    load_s = pltpu.make_async_copy(sizes, size_in, load_sem.at[3])
    load_t = pltpu.make_async_copy(taps, tap_in, load_sem.at[4])
    for load in (load_x, load_c, load_s, load_w, load_t):
        load.start()

    load_x.wait()
    for i in range(BLOCKS):
        x_all[zone * BLOCKS + i] = x_in[:, i * LANE : (i + 1) * LANE].astype(BF16)
    pl.semaphore_wait(barrier, n_zone - 1 + jnp.where(owner, 12, 1))
    mine = x_all.at[pl.ds(zone * BLOCKS, BLOCKS)]
    x_copies = []
    for peer in zone_order:
        step = lax.rem(peer - zone + n_zone, n_zone) - 1
        x_copies.append(
            pltpu.make_async_remote_copy(
                src_ref=mine,
                dst_ref=mine,
                send_sem=x_send.at[step],
                recv_sem=x_recv.at[step],
                device_id={"zone": peer},
                device_id_type=MESH,
            )
        )
        x_copies[-1].start()

    @pl.when(owner)
    def _():
        for step in (2, -2):
            greet(word.at[0], beside(step))

    @pl.when(jnp.logical_not(owner))
    def _():
        greet(word.at[2], host)

    load_s.wait()
    size_row = size_in[...].astype(F32)
    down, along = iota((LANE, LANE), 0), iota((LANE, LANE), 1)
    size_wide = jnp.broadcast_to(size_row, (LANE, LANE))
    size_tall = size_wide.T
    upto = jnp.sum(jnp.where(along <= down, size_wide, 0.0), axis=1, keepdims=True)
    before = jnp.sum(jnp.where(along < down, size_wide, 0.0), axis=1, keepdims=True)
    upto_row = jnp.sum(jnp.where(down <= along, size_tall, 0.0), axis=0, keepdims=True)
    before_row = jnp.sum(jnp.where(down < along, size_tall, 0.0), axis=0, keepdims=True)
    for i in range(BLOCKS):
        cell = (along + i * LANE).astype(F32)
        inside = (cell >= before) & (cell < upto)
        members[:, i * LANE : (i + 1) * LANE] = inside.astype(BF16)
        cell = (down + i * LANE).astype(F32)
        inside = (cell >= before_row) & (cell < upto_row)
        members_tall[i * LANE : (i + 1) * LANE, :] = inside.astype(BF16)

    @pl.when(owner)
    def _():
        pl.semaphore_wait(word.at[0], 2)
        for peer in lines:
            greet(word.at[1], peer)

    load_t.wait()
    load_c.wait()
    load_w.wait()
    for i in range(BLOCKS):
        for k in range(SLOTS):
            w_turned[i, k * LANE : (k + 1) * LANE, :] = w_all[i, k].T
    for copy in x_copies:
        copy.wait_recv()

    @pl.when(owner)
    def _():
        pl.semaphore_wait(word.at[1], 3)

    @pl.when(hosting)
    def _():
        pl.semaphore_wait(word.at[2], 2)
        for peer in guests:
            greet(word.at[3], peer)

    stress = []
    for i in range(BLOCKS):
        picked = jnp.concatenate([x_all[cols[k, i]] for k in range(SLOTS)], axis=1)
        wind = jnp.dot(picked, w_turned[i], preferred_element_type=F32)
        stress.append(wind * jnp.abs(wind))

    wide = jnp.concatenate(stress, axis=1)
    high, low = two_parts(wide)
    both = jnp.concatenate([high, low], axis=0)
    totals = jnp.dot(both, members_tall[...], preferred_element_type=F32)
    means = (totals[:SNAP] + totals[SNAP:]) / size_row
    high, low = two_parts(means)
    both = jnp.concatenate([high, low], axis=0)
    spread = jnp.dot(both, members[...], preferred_element_type=F32)
    anomaly = wide - spread[:SNAP] - spread[SNAP:]
    tiles = jnp.concatenate([anomaly[:, i * LANE : (i + 1) * LANE] for i in range(BLOCKS)], axis=0)

    def rows_wait(ref, rows, sem):
        part = ref.at[pl.ds(0, rows)]
        pltpu.make_async_copy(part, part, sem).wait()

    def rows_wait_owners(ref, each, sem):
        @pl.when(owner)
        def _():
            rows_wait(ref, each * (owners - 1), sem)

        @pl.when(jnp.logical_not(owner))
        def _():
            rows_wait(ref, each * owners, sem)

    turned = tiles.T
    first, second = turned[:owners], turned[owners:]
    odd = lax.rem(iota((owners, LANE), 1) // 4, 2) == 1
    send_a[pl.ds(0, owners, stride=2), :] = jnp.where(odd, pltpu.roll(second, 4, 1), first)
    send_a[pl.ds(1, owners, stride=2), :] = jnp.where(odd, second, pltpu.roll(first, LANE - 4, 1))

    def send_row(peer):
        pltpu.make_async_remote_copy(
            src_ref=send_a.at[pl.ds(2 * peer, 2)],
            dst_ref=recv_a.at[pl.ds(2 * tm, 2)],
            send_sem=a_send,
            recv_sem=a_recv,
            device_id={"tm": peer},
            device_id_type=MESH,
        ).start()

    steps = [(j, dq) for j in range(4) for dq in range(span)]
    steps.sort(key=lambda step: -((4, 3, 2, 3)[step[0]] + ring_distance(step[1] // cores, ring)))

    @pl.when(jnp.logical_not(owner))
    def _():
        pl.semaphore_wait(word.at[3], 1)

    for j, dq in steps:
        peer = lax.rem(tz + j, 4) * span + lax.rem(tq + dq, span)
        if j == 0 and dq == 0:
            pl.when(jnp.logical_not(owner))(functools.partial(send_row, peer))
        else:
            send_row(peer)

    @pl.when(owner)
    def _():
        recv_a[pl.ds(2 * tm, 2)] = send_a[pl.ds(2 * tm, 2)]

        pieces = []
        for q in range(8):
            row = tap_in[pl.ds(q * LANE - q // 7, LANE)].reshape(1, LANE)
            if q == 7:
                row = jnp.where(iota((1, LANE), 1) < LANE - 1, pltpu.roll(row, LANE - 1, 1), 0.0)
            row = jnp.broadcast_to(row, (8, LANE))
            pieces.append(jnp.where(lax.rem(iota((8, LANE), 1), 4) == iota((8, LANE), 0), row, 0.0))
        spread = jnp.concatenate(pieces, axis=1)
        pick = (iota((1024, 256), 0) // 4 == iota((1024, 256), 1)).astype(BF16)
        top, rest = two_parts(spread)
        last = (spread - top.astype(F32) - rest.astype(F32)).astype(BF16)
        by_phase = (
            jnp.dot(top, pick, preferred_element_type=F32)
            + jnp.dot(rest, pick, preferred_element_type=F32)
            + jnp.dot(last, pick, preferred_element_type=F32)
        )
        for n, (g, u) in enumerate(BANDS):
            phase, start = (3, 127) if g == 0 else (g - 1, 128)
            line = jnp.concatenate([by_phase[phase : phase + 1, :], jnp.zeros((1, 256), F32)], axis=1)
            wide = jnp.broadcast_to(line, (LANE, 512))
            high, low = two_parts(pltpu.roll(wide, (u - start) % 512, 1, stride=2, stride_axis=0)[:, :256])
            for slab, ref in zip(SLABS, toeplitz):
                rows, base = len(slab) * span, slab[0] * span
                ref[n * rows : (n + 1) * rows, :256] = high[base : base + rows]
                ref[n * rows : (n + 1) * rows, 256:] = low[base : base + rows]
        rows_wait(recv_a, 2 * n_tm - 2, a_recv)

        high, low = two_parts(recv_a[...])
        upper = jnp.concatenate([high, low], axis=1)
        lower = jnp.concatenate([high, jnp.zeros_like(high)], axis=1)
        right = jnp.concatenate([upper, lower], axis=0)

        def send_back(peer):
            pltpu.make_async_remote_copy(
                src_ref=send_b.at[pl.ds(2 * peer, 2)],
                dst_ref=recv_b.at[pl.ds(2 * tm, 2)],
                send_sem=b_send,
                recv_sem=b_recv,
                device_id={"tm": peer},
                device_id_type=MESH,
            ).start()

        for slab, ref in zip(SLABS, toeplitz):
            rows, base = len(slab) * span, slab[0] * span
            place = lax.rem(iota((rows, LANE), 1), 4)
            product = jnp.dot(ref[...], right, preferred_element_type=F32)
            product = product[:, :LANE] + product[:, LANE:]
            band = {b: product[n * rows : (n + 1) * rows] for n, b in enumerate(BANDS)}
            for u in range(2):
                total = band[0, u]
                for g in (1, 2, 3):
                    total += jnp.where(
                        place < 4 - g,
                        pltpu.roll(band[g, u], LANE - g, 1),
                        pltpu.roll(band[g, u + 1], 4 - g, 1),
                    )
                paired[pl.ds(2 * base + u, rows, stride=2), :] = total
            send_b[2 * base : 2 * (base + rows), :] = paired[2 * base : 2 * (base + rows), :].astype(BF16)
            for z in slab:
                for dq in sides:
                    peer = z * span + lax.rem(tq + dq, span)
                    if z < rings // 2 and dq == 0:
                        pl.when(tz != z)(functools.partial(send_back, peer))
                    else:
                        send_back(peer)
        here = pl.ds(2 * tm, 2)
        own = pltpu.make_async_copy(send_b.at[here], recv_b.at[here], load_sem.at[0])
        own.start()
        own.wait()

    n_pairs = BLOCKS * SLOTS
    all_blocks = BLOCKS * n_zone
    column_row = jnp.zeros((1, LANE), jnp.int32)
    lane = iota((1, LANE), 1)
    for i in range(BLOCKS):
        for k in range(SLOTS):
            column_row = jnp.where(lane == i * SLOTS + k, cols[k, i], column_row)
    chosen = (iota((all_blocks, LANE), 0) == column_row).astype(BF16)
    chosen = jnp.concatenate([chosen, chosen], axis=1)
    rows_wait_owners(recv_b, 2, b_recv)

    paired[: 2 * owners, :] = recv_b[...].astype(F32)
    even_row = paired[pl.ds(0, owners, stride=2), :]
    odd_row = paired[pl.ds(1, owners, stride=2), :]
    first = jnp.where(odd, pltpu.roll(odd_row, 4, 1), even_row)
    second = jnp.where(odd, odd_row, pltpu.roll(even_row, LANE - 4, 1))
    flow = jnp.concatenate([first, second], axis=0).T.astype(BF16)
    for i in range(BLOCKS):
        left = flow[i * SNAP : (i + 1) * SNAP, :]
        for k in range(0, SLOTS, 2):
            w_pair = jnp.concatenate([w_all[i, k], w_all[i, k + 1]], axis=1)
            pair = jnp.dot(left, w_pair, preferred_element_type=F32)
            base = (i * SLOTS + k) * SNAP
            contrib[base : base + SNAP, :] = pair[:, :LANE]
            contrib[base + SNAP : base + 2 * SNAP, :] = pair[:, LANE:]
    sums = []
    for t in range(0, SNAP, 2):
        sides = []
        for side in (t, t + 1):
            high, low = two_parts(contrib[pl.ds(side, n_pairs, stride=SNAP), :])
            sides.append(jnp.concatenate([high, low], axis=0))
        both = jnp.dot(chosen, jnp.concatenate(sides, axis=1), preferred_element_type=F32)
        sums += [both[:, :LANE], both[:, LANE:]]
    for t in range(SNAP):
        for z in range(n_zone):
            part = sums[t][z * BLOCKS : (z + 1) * BLOCKS]
            part_out[z, t] = part.astype(BF16)
            part_own[z, t] = part
    p_copies = []
    for n, peer in enumerate(zones):
        p_copies.append(
            pltpu.make_async_remote_copy(
                src_ref=part_out.at[peer],
                dst_ref=part_in.at[n],
                send_sem=p_send.at[n],
                recv_sem=p_recv.at[n],
                device_id={"zone": peer},
                device_id_type=MESH,
            )
        )
        p_copies[-1].start()
    for copy in x_copies:
        copy.wait_send()
    rows_wait_owners(send_a, 2, a_send)

    @pl.when(owner)
    def _():
        rows_wait(send_b, 2 * n_tm - 2, b_send)

    for copy in p_copies:
        copy.wait_recv()
    for t in range(SNAP):
        total = part_own[zone, t]
        for n in range(n_zone - 1):
            total += part_in[n, t].astype(F32)
        arranged[pl.ds(t, BLOCKS, stride=SNAP), :] = total
    for i in range(BLOCKS):
        out[:, i * LANE : (i + 1) * LANE] = arranged[i * SNAP : (i + 1) * SNAP, :]
    for copy in p_copies:
        copy.wait_send()


def solution(mesh):
    n_tm, n_zone = mesh.shape["tm"], mesh.shape["zone"]

    def shards(source_field, remap_weights, block_columns, piece_sizes, filter_taps):
        hbm = pl.BlockSpec(memory_space=pltpu.HBM)
        vmem = pl.BlockSpec(memory_space=pltpu.VMEM)
        dma = pltpu.SemaphoreType.DMA
        return pl.pallas_call(
            functools.partial(kernel, n_tm, n_zone),
            name="flux",
            out_shape=pltpu.VMEM(source_field.shape, F32),
            in_specs=[hbm] * 5,
            out_specs=vmem,
            scratch_shapes=[
                pltpu.VMEM(source_field.shape, F32),
                pltpu.VMEM((BLOCKS * n_zone, SNAP, LANE), BF16),
                pltpu.VMEM(remap_weights.shape, BF16),
                pltpu.VMEM((BLOCKS, SLOTS * LANE, LANE), BF16),
                pltpu.SMEM((SLOTS, BLOCKS), jnp.int32),
                pltpu.VMEM(piece_sizes.shape, jnp.int32),
                pltpu.VMEM(filter_taps.shape, F32),
                [pltpu.VMEM((len(BANDS) * len(slab) * 16, 512), BF16) for slab in SLABS],
                pltpu.VMEM((LANE, BLOCKS * LANE), BF16),
                pltpu.VMEM((BLOCKS * LANE, LANE), BF16),
                pltpu.VMEM((n_tm, LANE), F32),
                pltpu.VMEM((2 * n_tm, LANE), F32),
                pltpu.VMEM((2 * n_tm, LANE), BF16),
                pltpu.VMEM((n_tm, LANE), BF16),
                pltpu.VMEM((2 * n_tm, LANE), F32),
                pltpu.VMEM((BLOCKS * SLOTS * SNAP, LANE), F32),
                pltpu.VMEM((n_zone, SNAP, BLOCKS, LANE), BF16),
                pltpu.VMEM((n_zone - 1, SNAP, BLOCKS, LANE), BF16),
                pltpu.VMEM((n_zone, SNAP, BLOCKS, LANE), F32),
                pltpu.VMEM((BLOCKS * SNAP, LANE), F32),
                dma((5,)),
                dma((n_zone - 1,)),
                dma((n_zone - 1,)),
                dma,
                dma,
                dma,
                dma,
                dma((n_zone - 1,)),
                dma((n_zone - 1,)),
                pltpu.SemaphoreType.REGULAR((4,)),
            ],
            compiler_params=pltpu.CompilerParams(collective_id=0, has_side_effects=True),
        )(source_field, remap_weights, block_columns.T, piece_sizes, filter_taps)

    return jax.shard_map(
        shards,
        mesh=mesh,
        in_specs=(
            P("tm", "zone"),
            P("zone", None, None, None),
            P("zone", None),
            P("zone", None),
            P(),
        ),
        out_specs=P("tm", "zone"),
        check_vma=False,
    )
```

```python
import functools

import jax
import jax.numpy as jnp
from jax import lax
from jax.experimental import pallas as pl
from jax.experimental.pallas import tpu as pltpu
from jax.sharding import PartitionSpec as P

MESH = pl.DeviceIdType.MESH
F32 = jnp.float32
BF16 = jnp.bfloat16
SNAP = 8
LANE = 128
BLOCKS = 16
SLOTS = 8
SLABS = [(0, 1), (2, 3), (4, 5, 6, 7)]
BANDS = [(0, 0), (0, 1)] + [(g, u) for g in (1, 2, 3) for u in (0, 1, 2)]


def iota(shape, dim):
    return lax.broadcasted_iota(jnp.int32, shape, dim)


def two_parts(value):
    high = value.astype(BF16)
    low = (value - high.astype(F32)).astype(BF16)
    return high, low


def ring_distance(offset, length):
    return min(offset, length - offset)


def kernel(
    n_tm,
    n_zone,
    source,
    weights,
    columns,
    sizes,
    taps,
    out,
    x_in,
    x_all,
    w_all,
    w_turned,
    cols,
    size_in,
    tap_in,
    toeplitz,
    members,
    members_tall,
    send_a,
    recv_a,
    send_b,
    recv_b,
    paired,
    contrib,
    part_out,
    part_in,
    part_own,
    arranged,
    load_sem,
    x_send,
    x_recv,
    a_send,
    a_recv,
    b_send,
    b_recv,
    p_send,
    p_recv,
    word,
):
    tm = lax.axis_index("tm")
    zone = lax.axis_index("zone")
    rings, ring, cores = 8, 8, 2
    span = ring * cores
    owners = n_tm // 2
    tz, tq = tm // span, lax.rem(tm, span)
    owner = tm < owners
    sides = sorted(range(span), key=lambda dq: -ring_distance(dq // cores, ring))
    zones = [lax.rem(zone + step, n_zone) for step in (2, 1, 3)]

    core = lax.rem(tq, cores)

    def beside(step):
        return tz * span + lax.rem(tq + step * cores + span, span)

    def greet(semaphore, peer):
        pl.semaphore_signal(semaphore, inc=1, device_id={"tm": peer}, device_id_type=MESH)

    zone_order = [
        jnp.where(zone == 2, 1, 2),
        jnp.where((zone == 1) | (zone == 2), 3, 1),
        jnp.where(zone == 0, 3, 0),
    ]

    barrier = pltpu.get_barrier_semaphore()
    for peer in zones:
        pl.semaphore_signal(barrier, inc=1, device_id={"zone": peer}, device_id_type=MESH)
    lines = [lax.rem(tz + dz, 4) * span + tq for dz in (1, 2, 3)]
    host = jnp.where(tz < 6, 3, 0) * span + tq
    hosting = (tz == 0) | (tz == 3)
    guests = [jnp.where(tz == 0, far, near) * span + tq for far, near in ((7, 4), (6, 5))]

    @pl.when(owner)
    def _():
        for step in (2, -2, 1, -1):
            greet(barrier, beside(step))
            greet(barrier, beside(step) + 1 - 2 * core)
        greet(barrier, tm + 1 - 2 * core)
        for peer in lines:
            greet(barrier, peer)

    @pl.when(hosting)
    def _():
        for peer in guests:
            greet(barrier, peer)

    load_x = pltpu.make_async_copy(source, x_in, load_sem.at[0])
    load_c = pltpu.make_async_copy(columns, cols, load_sem.at[1])
    load_w = pltpu.make_async_copy(weights, w_all, load_sem.at[2])
    load_s = pltpu.make_async_copy(sizes, size_in, load_sem.at[3])
    load_t = pltpu.make_async_copy(taps, tap_in, load_sem.at[4])
    for load in (load_x, load_c, load_s, load_w, load_t):
        load.start()

    load_x.wait()
    for i in range(BLOCKS):
        x_all[zone * BLOCKS + i] = x_in[:, i * LANE : (i + 1) * LANE].astype(BF16)
    pl.semaphore_wait(barrier, n_zone - 1 + jnp.where(owner, 12, 1))
    mine = x_all.at[pl.ds(zone * BLOCKS, BLOCKS)]
    x_copies = []
    for peer in zone_order:
        step = lax.rem(peer - zone + n_zone, n_zone) - 1
        x_copies.append(
            pltpu.make_async_remote_copy(
                src_ref=mine,
                dst_ref=mine,
                send_sem=x_send.at[step],
                recv_sem=x_recv.at[step],
                device_id={"zone": peer},
                device_id_type=MESH,
            )
        )
        x_copies[-1].start()

    @pl.when(owner)
    def _():
        for step in (2, -2):
            greet(word.at[0], beside(step))

    @pl.when(jnp.logical_not(owner))
    def _():
        greet(word.at[2], host)

    load_s.wait()
    size_row = size_in[...].astype(F32)
    down, along = iota((LANE, LANE), 0), iota((LANE, LANE), 1)
    size_wide = jnp.broadcast_to(size_row, (LANE, LANE))
    size_tall = size_wide.T
    upto = jnp.sum(jnp.where(along <= down, size_wide, 0.0), axis=1, keepdims=True)
    before = jnp.sum(jnp.where(along < down, size_wide, 0.0), axis=1, keepdims=True)
    upto_row = jnp.sum(jnp.where(down <= along, size_tall, 0.0), axis=0, keepdims=True)
    before_row = jnp.sum(jnp.where(down < along, size_tall, 0.0), axis=0, keepdims=True)
    for i in range(BLOCKS):
        cell = (along + i * LANE).astype(F32)
        inside = (cell >= before) & (cell < upto)
        members[:, i * LANE : (i + 1) * LANE] = inside.astype(BF16)
        cell = (down + i * LANE).astype(F32)
        inside = (cell >= before_row) & (cell < upto_row)
        members_tall[i * LANE : (i + 1) * LANE, :] = inside.astype(BF16)

    @pl.when(owner)
    def _():
        pl.semaphore_wait(word.at[0], 2)
        for peer in lines:
            greet(word.at[1], peer)

    load_t.wait()
    load_c.wait()
    load_w.wait()
    for i in range(BLOCKS):
        for k in range(SLOTS):
            w_turned[i, k * LANE : (k + 1) * LANE, :] = w_all[i, k].T
    for copy in x_copies:
        copy.wait_recv()

    @pl.when(owner)
    def _():
        pl.semaphore_wait(word.at[1], 3)

    @pl.when(hosting)
    def _():
        pl.semaphore_wait(word.at[2], 2)
        for peer in guests:
            greet(word.at[3], peer)

    stress = []
    for i in range(BLOCKS):
        picked = jnp.concatenate([x_all[cols[k, i]] for k in range(SLOTS)], axis=1)
        wind = jnp.dot(picked, w_turned[i], preferred_element_type=F32)
        stress.append(wind * jnp.abs(wind))

    wide = jnp.concatenate(stress, axis=1)
    high, low = two_parts(wide)
    both = jnp.concatenate([high, low], axis=0)
    totals = jnp.dot(both, members_tall[...], preferred_element_type=F32)
    means = (totals[:SNAP] + totals[SNAP:]) / size_row
    high, low = two_parts(means)
    both = jnp.concatenate([high, low], axis=0)
    spread = jnp.dot(both, members[...], preferred_element_type=F32)
    anomaly = wide - spread[:SNAP] - spread[SNAP:]
    tiles = jnp.concatenate([anomaly[:, i * LANE : (i + 1) * LANE] for i in range(BLOCKS)], axis=0)

    def rows_wait(ref, rows, sem):
        part = ref.at[pl.ds(0, rows)]
        pltpu.make_async_copy(part, part, sem).wait()

    def rows_wait_owners(ref, sem):
        @pl.when(owner)
        def _():
            rows_wait(ref, 2 * owners - 2, sem)

        @pl.when(jnp.logical_not(owner))
        def _():
            rows_wait(ref, 2 * owners, sem)

    turned = tiles.T
    first, second = turned[:owners], turned[owners:]
    odd = lax.rem(iota((owners, LANE), 1) // 4, 2) == 1
    send_a[pl.ds(0, owners, stride=2), :] = jnp.where(odd, pltpu.roll(second, 4, 1), first)
    send_a[pl.ds(1, owners, stride=2), :] = jnp.where(odd, second, pltpu.roll(first, LANE - 4, 1))

    def send_row(peer):
        pltpu.make_async_remote_copy(
            src_ref=send_a.at[pl.ds(2 * peer, 2)],
            dst_ref=recv_a.at[pl.ds(2 * tm, 2)],
            send_sem=a_send,
            recv_sem=a_recv,
            device_id={"tm": peer},
            device_id_type=MESH,
        ).start()

    steps = [(j, dq) for j in range(4) for dq in range(span)]
    steps.sort(key=lambda step: -((4, 3, 2, 3)[step[0]] + ring_distance(step[1] // cores, ring)))

    @pl.when(jnp.logical_not(owner))
    def _():
        pl.semaphore_wait(word.at[3], 1)

    for j, dq in steps:
        peer = lax.rem(tz + j, 4) * span + lax.rem(tq + dq, span)
        if j == 0 and dq == 0:
            pl.when(jnp.logical_not(owner))(functools.partial(send_row, peer))
        else:
            send_row(peer)

    @pl.when(owner)
    def _():
        recv_a[pl.ds(2 * tm, 2)] = send_a[pl.ds(2 * tm, 2)]

        pieces = []
        for q in range(8):
            row = tap_in[pl.ds(q * LANE - q // 7, LANE)].reshape(1, LANE)
            if q == 7:
                row = jnp.where(iota((1, LANE), 1) < LANE - 1, pltpu.roll(row, LANE - 1, 1), 0.0)
            row = jnp.broadcast_to(row, (8, LANE))
            pieces.append(jnp.where(lax.rem(iota((8, LANE), 1), 4) == iota((8, LANE), 0), row, 0.0))
        spread = jnp.concatenate(pieces, axis=1)
        pick = (iota((1024, 256), 0) // 4 == iota((1024, 256), 1)).astype(BF16)
        top, rest = two_parts(spread)
        last = (spread - top.astype(F32) - rest.astype(F32)).astype(BF16)
        by_phase = (
            jnp.dot(top, pick, preferred_element_type=F32)
            + jnp.dot(rest, pick, preferred_element_type=F32)
            + jnp.dot(last, pick, preferred_element_type=F32)
        )
        for n, (g, u) in enumerate(BANDS):
            phase, start = (3, 127) if g == 0 else (g - 1, 128)
            line = jnp.concatenate([by_phase[phase : phase + 1, :], jnp.zeros((1, 256), F32)], axis=1)
            wide = jnp.broadcast_to(line, (LANE, 512))
            high, low = two_parts(pltpu.roll(wide, (u - start) % 512, 1, stride=2, stride_axis=0)[:, :256])
            for slab, ref in zip(SLABS, toeplitz):
                rows, base = len(slab) * span, slab[0] * span
                ref[n * rows : (n + 1) * rows, :256] = high[base : base + rows]
                ref[n * rows : (n + 1) * rows, 256:] = low[base : base + rows]
        rows_wait(recv_a, 2 * n_tm - 2, a_recv)

        high, low = two_parts(recv_a[...])
        upper = jnp.concatenate([high, low], axis=1)
        lower = jnp.concatenate([high, jnp.zeros_like(high)], axis=1)
        right = jnp.concatenate([upper, lower], axis=0)

        def send_back(peer):
            pltpu.make_async_remote_copy(
                src_ref=send_b.at[pl.ds(2 * peer, 2)],
                dst_ref=recv_b.at[pl.ds(2 * tm, 2)],
                send_sem=b_send,
                recv_sem=b_recv.at[tz // 2],
                device_id={"tm": peer},
                device_id_type=MESH,
            ).start()

        for slab, ref in zip(SLABS, toeplitz):
            rows, base = len(slab) * span, slab[0] * span
            place = lax.rem(iota((rows, LANE), 1), 4)
            product = jnp.dot(ref[...], right, preferred_element_type=F32)
            product = product[:, :LANE] + product[:, LANE:]
            band = {b: product[n * rows : (n + 1) * rows] for n, b in enumerate(BANDS)}
            for u in range(2):
                total = band[0, u]
                for g in (1, 2, 3):
                    total += jnp.where(
                        place < 4 - g,
                        pltpu.roll(band[g, u], LANE - g, 1),
                        pltpu.roll(band[g, u + 1], 4 - g, 1),
                    )
                paired[pl.ds(2 * base + u, rows, stride=2), :] = total
            send_b[2 * base : 2 * (base + rows), :] = paired[2 * base : 2 * (base + rows), :].astype(BF16)
            for z in slab:
                for dq in sides:
                    peer = z * span + lax.rem(tq + dq, span)
                    if z < rings // 2 and dq == 0:
                        pl.when(tz != z)(functools.partial(send_back, peer))
                    else:
                        send_back(peer)
        here = pl.ds(2 * tm, 2)
        own = pltpu.make_async_copy(send_b.at[here], recv_b.at[here], load_sem.at[0])
        own.start()
        own.wait()

    n_pairs = BLOCKS * SLOTS
    all_blocks = BLOCKS * n_zone
    column_row = jnp.zeros((1, LANE), jnp.int32)
    lane = iota((1, LANE), 1)
    for i in range(BLOCKS):
        for k in range(SLOTS):
            column_row = jnp.where(lane == i * SLOTS + k, cols[k, i], column_row)
    chosen = (iota((all_blocks, LANE), 0) == column_row).astype(BF16)
    chosen = jnp.concatenate([chosen, chosen], axis=1)

    quarter = owners // 2
    odd = lax.rem(iota((quarter, LANE), 1) // 4, 2) == 1
    for part in range(2):
        mine_too = owner & (tz // 2 == part)
        from_rows = recv_b.at[pl.ds(owners * part, owners)]
        but_mine = recv_b.at[pl.ds(owners * part, owners - 2)]

        @pl.when(mine_too)
        def _():
            pltpu.make_async_copy(but_mine, but_mine, b_recv.at[part]).wait()

        @pl.when(jnp.logical_not(mine_too))
        def _():
            pltpu.make_async_copy(from_rows, from_rows, b_recv.at[part]).wait()

        paired[part * owners : (part + 1) * owners, :] = recv_b[part * owners : (part + 1) * owners, :].astype(F32)
        even_row = paired[pl.ds(part * owners, quarter, stride=2), :]
        odd_row = paired[pl.ds(part * owners + 1, quarter, stride=2), :]
        first = jnp.where(odd, pltpu.roll(odd_row, 4, 1), even_row)
        second = jnp.where(odd, odd_row, pltpu.roll(even_row, LANE - 4, 1))
        flow = jnp.concatenate([first, second], axis=0).T.astype(BF16)
        low_a, high_a = part * quarter, owners + part * quarter
        for i in range(BLOCKS):
            left = flow[i * SNAP : (i + 1) * SNAP, :]
            for k in range(0, SLOTS, 2):
                w_low = [w_all[i, n, low_a : low_a + quarter, :] for n in (k, k + 1)]
                w_high = [w_all[i, n, high_a : high_a + quarter, :] for n in (k, k + 1)]
                w_pair = jnp.concatenate(
                    [jnp.concatenate(w_low, axis=1), jnp.concatenate(w_high, axis=1)], axis=0
                )
                pair = jnp.dot(left, w_pair, preferred_element_type=F32)
                for n in range(2):
                    base = (i * SLOTS + k + n) * SNAP
                    term = pair[:, n * LANE : (n + 1) * LANE]
                    if part == 0:
                        contrib[base : base + SNAP, :] = term
                    else:
                        contrib[base : base + SNAP, :] += term
    sums = []
    for t in range(0, SNAP, 2):
        sides = []
        for side in (t, t + 1):
            high, low = two_parts(contrib[pl.ds(side, n_pairs, stride=SNAP), :])
            sides.append(jnp.concatenate([high, low], axis=0))
        both = jnp.dot(chosen, jnp.concatenate(sides, axis=1), preferred_element_type=F32)
        sums += [both[:, :LANE], both[:, LANE:]]
    for t in range(SNAP):
        for z in range(n_zone):
            part = sums[t][z * BLOCKS : (z + 1) * BLOCKS]
            part_out[z, t] = part.astype(BF16)
            part_own[z, t] = part
    p_copies = []
    for n, peer in enumerate(zones):
        p_copies.append(
            pltpu.make_async_remote_copy(
                src_ref=part_out.at[peer],
                dst_ref=part_in.at[n],
                send_sem=p_send.at[n],
                recv_sem=p_recv.at[n],
                device_id={"zone": peer},
                device_id_type=MESH,
            )
        )
        p_copies[-1].start()
    for copy in x_copies:
        copy.wait_send()
    rows_wait_owners(send_a, a_send)

    @pl.when(owner)
    def _():
        rows_wait(send_b, 2 * n_tm - 2, b_send)

    for copy in p_copies:
        copy.wait_recv()
    for t in range(SNAP):
        total = part_own[zone, t]
        for n in range(n_zone - 1):
            total += part_in[n, t].astype(F32)
        arranged[pl.ds(t, BLOCKS, stride=SNAP), :] = total
    for i in range(BLOCKS):
        out[:, i * LANE : (i + 1) * LANE] = arranged[i * SNAP : (i + 1) * SNAP, :]
    for copy in p_copies:
        copy.wait_send()


def solution(mesh):
    n_tm, n_zone = mesh.shape["tm"], mesh.shape["zone"]

    def shards(source_field, remap_weights, block_columns, piece_sizes, filter_taps):
        hbm = pl.BlockSpec(memory_space=pltpu.HBM)
        vmem = pl.BlockSpec(memory_space=pltpu.VMEM)
        dma = pltpu.SemaphoreType.DMA
        return pl.pallas_call(
            functools.partial(kernel, n_tm, n_zone),
            name="flux",
            out_shape=pltpu.VMEM(source_field.shape, F32),
            in_specs=[hbm] * 5,
            out_specs=vmem,
            scratch_shapes=[
                pltpu.VMEM(source_field.shape, F32),
                pltpu.VMEM((BLOCKS * n_zone, SNAP, LANE), BF16),
                pltpu.VMEM(remap_weights.shape, BF16),
                pltpu.VMEM((BLOCKS, SLOTS * LANE, LANE), BF16),
                pltpu.SMEM((SLOTS, BLOCKS), jnp.int32),
                pltpu.VMEM(piece_sizes.shape, jnp.int32),
                pltpu.VMEM(filter_taps.shape, F32),
                [pltpu.VMEM((len(BANDS) * len(slab) * 16, 512), BF16) for slab in SLABS],
                pltpu.VMEM((LANE, BLOCKS * LANE), BF16),
                pltpu.VMEM((BLOCKS * LANE, LANE), BF16),
                pltpu.VMEM((n_tm, LANE), F32),
                pltpu.VMEM((2 * n_tm, LANE), F32),
                pltpu.VMEM((2 * n_tm, LANE), BF16),
                pltpu.VMEM((n_tm, LANE), BF16),
                pltpu.VMEM((2 * n_tm, LANE), F32),
                pltpu.VMEM((BLOCKS * SLOTS * SNAP, LANE), F32),
                pltpu.VMEM((n_zone, SNAP, BLOCKS, LANE), BF16),
                pltpu.VMEM((n_zone - 1, SNAP, BLOCKS, LANE), BF16),
                pltpu.VMEM((n_zone, SNAP, BLOCKS, LANE), F32),
                pltpu.VMEM((BLOCKS * SNAP, LANE), F32),
                dma((5,)),
                dma((n_zone - 1,)),
                dma((n_zone - 1,)),
                dma,
                dma,
                dma,
                dma((2,)),
                dma((n_zone - 1,)),
                dma((n_zone - 1,)),
                pltpu.SemaphoreType.REGULAR((4,)),
            ],
            compiler_params=pltpu.CompilerParams(collective_id=0, has_side_effects=True),
        )(source_field, remap_weights, block_columns.T, piece_sizes, filter_taps)

    return jax.shard_map(
        shards,
        mesh=mesh,
        in_specs=(
            P("tm", "zone"),
            P("zone", None, None, None),
            P("zone", None),
            P("zone", None),
            P(),
        ),
        out_specs=P("tm", "zone"),
        check_vma=False,
    )
```

```python
import functools

import jax
import jax.numpy as jnp
from jax import lax
from jax.experimental import pallas as pl
from jax.experimental.pallas import tpu as pltpu
from jax.sharding import PartitionSpec as P

MESH = pl.DeviceIdType.MESH
F32 = jnp.float32
BF16 = jnp.bfloat16
SNAP = 8
LANE = 128
BLOCKS = 16
SLOTS = 8
SLABS = [(0, 1), (2, 3), (4, 5, 6, 7)]
BANDS = [(0, 0), (0, 1)] + [(g, u) for g in (1, 2, 3) for u in (0, 1, 2)]


def iota(shape, dim):
    return lax.broadcasted_iota(jnp.int32, shape, dim)


def two_parts(value):
    high = value.astype(BF16)
    low = (value - high.astype(F32)).astype(BF16)
    return high, low


def ring_distance(offset, length):
    return min(offset, length - offset)


def kernel(
    n_tm,
    n_zone,
    source,
    weights,
    columns,
    sizes,
    taps,
    out,
    x_in,
    x_all,
    w_all,
    w_turned,
    cols,
    size_in,
    tap_in,
    toeplitz,
    members,
    members_tall,
    send_a,
    recv_a,
    send_b,
    recv_b,
    paired,
    contrib,
    part_out,
    part_in,
    part_own,
    arranged,
    load_sem,
    x_send,
    x_recv,
    a_send,
    a_recv,
    b_send,
    b_recv,
    p_send,
    p_recv,
    word,
):
    tm = lax.axis_index("tm")
    zone = lax.axis_index("zone")
    rings, ring, cores = 8, 8, 2
    span = ring * cores
    owners = n_tm // 2
    tz, tq = tm // span, lax.rem(tm, span)
    owner = tm < owners
    sides = sorted(range(span), key=lambda dq: -ring_distance(dq // cores, ring))
    zones = [lax.rem(zone + step, n_zone) for step in (2, 1, 3)]

    core = lax.rem(tq, cores)

    def beside(step):
        return tz * span + lax.rem(tq + step * cores + span, span)

    def greet(semaphore, peer):
        pl.semaphore_signal(semaphore, inc=1, device_id={"tm": peer}, device_id_type=MESH)

    zone_order = [
        jnp.where(zone == 2, 1, 2),
        jnp.where((zone == 1) | (zone == 2), 3, 1),
        jnp.where(zone == 0, 3, 0),
    ]

    barrier = pltpu.get_barrier_semaphore()
    for peer in zones:
        pl.semaphore_signal(barrier, inc=1, device_id={"zone": peer}, device_id_type=MESH)
    lines = [lax.rem(tz + dz, 4) * span + tq for dz in (1, 2, 3)]
    host = jnp.where(tz < 6, 3, 0) * span + tq
    hosting = (tz == 0) | (tz == 3)
    guests = [jnp.where(tz == 0, far, near) * span + tq for far, near in ((7, 4), (6, 5))]

    @pl.when(owner)
    def _():
        for step in (2, -2, 1, -1):
            greet(barrier, beside(step))
            greet(barrier, beside(step) + 1 - 2 * core)
        greet(barrier, tm + 1 - 2 * core)
        for peer in lines:
            greet(barrier, peer)

    @pl.when(hosting)
    def _():
        for peer in guests:
            greet(barrier, peer)

    load_x = pltpu.make_async_copy(source, x_in, load_sem.at[0])
    load_c = pltpu.make_async_copy(columns, cols, load_sem.at[1])
    load_w = pltpu.make_async_copy(weights, w_all, load_sem.at[2])
    load_s = pltpu.make_async_copy(sizes, size_in, load_sem.at[3])
    load_t = pltpu.make_async_copy(taps, tap_in, load_sem.at[4])
    for load in (load_x, load_c, load_s, load_w, load_t):
        load.start()

    load_x.wait()
    for i in range(BLOCKS):
        x_all[zone * BLOCKS + i] = x_in[:, i * LANE : (i + 1) * LANE].astype(BF16)
    pl.semaphore_wait(barrier, n_zone - 1 + jnp.where(owner, 12, 1))
    mine = x_all.at[pl.ds(zone * BLOCKS, BLOCKS)]
    x_copies = []
    for peer in zone_order:
        step = lax.rem(peer - zone + n_zone, n_zone) - 1
        x_copies.append(
            pltpu.make_async_remote_copy(
                src_ref=mine,
                dst_ref=mine,
                send_sem=x_send.at[step],
                recv_sem=x_recv.at[step],
                device_id={"zone": peer},
                device_id_type=MESH,
            )
        )
        x_copies[-1].start()

    @pl.when(owner)
    def _():
        for step in (2, -2):
            greet(word.at[0], beside(step))

    @pl.when(jnp.logical_not(owner))
    def _():
        greet(word.at[2], host)

    load_s.wait()
    size_row = size_in[...].astype(F32)
    down, along = iota((LANE, LANE), 0), iota((LANE, LANE), 1)
    size_wide = jnp.broadcast_to(size_row, (LANE, LANE))
    size_tall = size_wide.T
    upto = jnp.sum(jnp.where(along <= down, size_wide, 0.0), axis=1, keepdims=True)
    before = jnp.sum(jnp.where(along < down, size_wide, 0.0), axis=1, keepdims=True)
    upto_row = jnp.sum(jnp.where(down <= along, size_tall, 0.0), axis=0, keepdims=True)
    before_row = jnp.sum(jnp.where(down < along, size_tall, 0.0), axis=0, keepdims=True)
    for i in range(BLOCKS):
        cell = (along + i * LANE).astype(F32)
        inside = (cell >= before) & (cell < upto)
        members[:, i * LANE : (i + 1) * LANE] = inside.astype(BF16)
        cell = (down + i * LANE).astype(F32)
        inside = (cell >= before_row) & (cell < upto_row)
        members_tall[i * LANE : (i + 1) * LANE, :] = inside.astype(BF16)

    @pl.when(owner)
    def _():
        pl.semaphore_wait(word.at[0], 2)
        for peer in lines:
            greet(word.at[1], peer)

    load_t.wait()
    load_c.wait()
    load_w.wait()
    for i in range(BLOCKS):
        for k in range(SLOTS):
            w_turned[i, k * LANE : (k + 1) * LANE, :] = w_all[i, k].T
    for copy in x_copies:
        copy.wait_recv()

    @pl.when(owner)
    def _():
        pl.semaphore_wait(word.at[1], 3)

    @pl.when(hosting)
    def _():
        pl.semaphore_wait(word.at[2], 2)
        for peer in guests:
            greet(word.at[3], peer)

    stress = []
    for i in range(BLOCKS):
        picked = jnp.concatenate([x_all[cols[k, i]] for k in range(SLOTS)], axis=1)
        wind = jnp.dot(picked, w_turned[i], preferred_element_type=F32)
        stress.append(wind * jnp.abs(wind))

    wide = jnp.concatenate(stress, axis=1)
    high, low = two_parts(wide)
    both = jnp.concatenate([high, low], axis=0)
    totals = jnp.dot(both, members_tall[...], preferred_element_type=F32)
    means = (totals[:SNAP] + totals[SNAP:]) / size_row
    high, low = two_parts(means)
    both = jnp.concatenate([high, low], axis=0)
    spread = jnp.dot(both, members[...], preferred_element_type=F32)
    anomaly = wide - spread[:SNAP] - spread[SNAP:]
    tiles = jnp.concatenate([anomaly[:, i * LANE : (i + 1) * LANE] for i in range(BLOCKS)], axis=0)

    def rows_wait(ref, rows, sem):
        part = ref.at[pl.ds(0, rows)]
        pltpu.make_async_copy(part, part, sem).wait()

    def rows_wait_owners(ref, sem):
        @pl.when(owner)
        def _():
            rows_wait(ref, 2 * owners - 2, sem)

        @pl.when(jnp.logical_not(owner))
        def _():
            rows_wait(ref, 2 * owners, sem)

    turned = tiles.T
    first, second = turned[:owners], turned[owners:]
    odd = lax.rem(iota((owners, LANE), 1) // 4, 2) == 1
    send_a[pl.ds(0, owners, stride=2), :] = jnp.where(odd, pltpu.roll(second, 4, 1), first)
    send_a[pl.ds(1, owners, stride=2), :] = jnp.where(odd, second, pltpu.roll(first, LANE - 4, 1))

    def send_row(peer):
        pltpu.make_async_remote_copy(
            src_ref=send_a.at[pl.ds(2 * peer, 2)],
            dst_ref=recv_a.at[pl.ds(2 * tm, 2)],
            send_sem=a_send,
            recv_sem=a_recv,
            device_id={"tm": peer},
            device_id_type=MESH,
        ).start()

    steps = [(j, dq) for j in range(4) for dq in range(span)]
    steps.sort(key=lambda step: -((4, 3, 2, 3)[step[0]] + ring_distance(step[1] // cores, ring)))

    @pl.when(jnp.logical_not(owner))
    def _():
        pl.semaphore_wait(word.at[3], 1)

    for j, dq in steps:
        peer = lax.rem(tz + j, 4) * span + lax.rem(tq + dq, span)
        if j == 0 and dq == 0:
            pl.when(jnp.logical_not(owner))(functools.partial(send_row, peer))
        else:
            send_row(peer)

    @pl.when(owner)
    def _():
        recv_a[pl.ds(2 * tm, 2)] = send_a[pl.ds(2 * tm, 2)]

        pieces = []
        for q in range(8):
            row = tap_in[pl.ds(q * LANE - q // 7, LANE)].reshape(1, LANE)
            if q == 7:
                row = jnp.where(iota((1, LANE), 1) < LANE - 1, pltpu.roll(row, LANE - 1, 1), 0.0)
            row = jnp.broadcast_to(row, (8, LANE))
            pieces.append(jnp.where(lax.rem(iota((8, LANE), 1), 4) == iota((8, LANE), 0), row, 0.0))
        spread = jnp.concatenate(pieces, axis=1)
        pick = (iota((1024, 256), 0) // 4 == iota((1024, 256), 1)).astype(BF16)
        top, rest = two_parts(spread)
        last = (spread - top.astype(F32) - rest.astype(F32)).astype(BF16)
        by_phase = (
            jnp.dot(top, pick, preferred_element_type=F32)
            + jnp.dot(rest, pick, preferred_element_type=F32)
            + jnp.dot(last, pick, preferred_element_type=F32)
        )
        for n, (g, u) in enumerate(BANDS):
            phase, start = (3, 127) if g == 0 else (g - 1, 128)
            line = jnp.concatenate([by_phase[phase : phase + 1, :], jnp.zeros((1, 256), F32)], axis=1)
            wide = jnp.broadcast_to(line, (LANE, 512))
            high, low = two_parts(pltpu.roll(wide, (u - start) % 512, 1, stride=2, stride_axis=0)[:, :256])
            for slab, ref in zip(SLABS, toeplitz):
                rows, base = len(slab) * span, slab[0] * span
                ref[n * rows : (n + 1) * rows, :256] = high[base : base + rows]
                ref[n * rows : (n + 1) * rows, 256:] = low[base : base + rows]
        rows_wait(recv_a, 2 * n_tm - 2, a_recv)

        high, low = two_parts(recv_a[...])
        upper = jnp.concatenate([high, low], axis=1)
        lower = jnp.concatenate([high, jnp.zeros_like(high)], axis=1)
        right = jnp.concatenate([upper, lower], axis=0)

        def send_back(peer):
            pltpu.make_async_remote_copy(
                src_ref=send_b.at[pl.ds(2 * peer, 2)],
                dst_ref=recv_b.at[pl.ds(2 * tm, 2)],
                send_sem=b_send,
                recv_sem=b_recv.at[tz],
                device_id={"tm": peer},
                device_id_type=MESH,
            ).start()

        for slab, ref in zip(SLABS, toeplitz):
            rows, base = len(slab) * span, slab[0] * span
            place = lax.rem(iota((rows, LANE), 1), 4)
            product = jnp.dot(ref[...], right, preferred_element_type=F32)
            product = product[:, :LANE] + product[:, LANE:]
            band = {b: product[n * rows : (n + 1) * rows] for n, b in enumerate(BANDS)}
            for u in range(2):
                total = band[0, u]
                for g in (1, 2, 3):
                    total += jnp.where(
                        place < 4 - g,
                        pltpu.roll(band[g, u], LANE - g, 1),
                        pltpu.roll(band[g, u + 1], 4 - g, 1),
                    )
                paired[pl.ds(2 * base + u, rows, stride=2), :] = total
            send_b[2 * base : 2 * (base + rows), :] = paired[2 * base : 2 * (base + rows), :].astype(BF16)
            for z in slab:
                for dq in sides:
                    peer = z * span + lax.rem(tq + dq, span)
                    if z < rings // 2 and dq == 0:
                        pl.when(tz != z)(functools.partial(send_back, peer))
                    else:
                        send_back(peer)
        here = pl.ds(2 * tm, 2)
        own = pltpu.make_async_copy(send_b.at[here], recv_b.at[here], load_sem.at[0])
        own.start()
        own.wait()

    n_pairs = BLOCKS * SLOTS
    all_blocks = BLOCKS * n_zone
    column_row = jnp.zeros((1, LANE), jnp.int32)
    lane = iota((1, LANE), 1)
    for i in range(BLOCKS):
        for k in range(SLOTS):
            column_row = jnp.where(lane == i * SLOTS + k, cols[k, i], column_row)
    chosen = (iota((all_blocks, LANE), 0) == column_row).astype(BF16)
    chosen = jnp.concatenate([chosen, chosen], axis=1)

    quarter = owners // 4
    strip = 2 * quarter
    odd = lax.rem(iota((quarter, LANE), 1) // 4, 2) == 1
    for part in range(4):
        mine_too = tz == part
        from_rows = recv_b.at[pl.ds(strip * part, strip)]
        but_mine = recv_b.at[pl.ds(strip * part, strip - 2)]

        @pl.when(mine_too)
        def _():
            pltpu.make_async_copy(but_mine, but_mine, b_recv.at[part]).wait()

        @pl.when(jnp.logical_not(mine_too))
        def _():
            pltpu.make_async_copy(from_rows, from_rows, b_recv.at[part]).wait()

        paired[part * strip : (part + 1) * strip, :] = recv_b[part * strip : (part + 1) * strip, :].astype(F32)
        even_row = paired[pl.ds(part * strip, quarter, stride=2), :]
        odd_row = paired[pl.ds(part * strip + 1, quarter, stride=2), :]
        first = jnp.where(odd, pltpu.roll(odd_row, 4, 1), even_row)
        second = jnp.where(odd, odd_row, pltpu.roll(even_row, LANE - 4, 1))
        flow = jnp.concatenate([first, second], axis=0).T.astype(BF16)
        low_a, high_a = part * quarter, owners + part * quarter
        for i in range(BLOCKS):
            left = flow[i * SNAP : (i + 1) * SNAP, :]
            for k in range(0, SLOTS, 2):
                w_low = [w_all[i, n, low_a : low_a + quarter, :] for n in (k, k + 1)]
                w_high = [w_all[i, n, high_a : high_a + quarter, :] for n in (k, k + 1)]
                w_pair = jnp.concatenate(
                    [jnp.concatenate(w_low, axis=1), jnp.concatenate(w_high, axis=1)], axis=0
                )
                pair = jnp.dot(left, w_pair, preferred_element_type=F32)
                for n in range(2):
                    base = (i * SLOTS + k + n) * SNAP
                    term = pair[:, n * LANE : (n + 1) * LANE]
                    if part == 0:
                        contrib[base : base + SNAP, :] = term
                    else:
                        contrib[base : base + SNAP, :] += term
    sums = []
    for t in range(0, SNAP, 2):
        sides = []
        for side in (t, t + 1):
            high, low = two_parts(contrib[pl.ds(side, n_pairs, stride=SNAP), :])
            sides.append(jnp.concatenate([high, low], axis=0))
        both = jnp.dot(chosen, jnp.concatenate(sides, axis=1), preferred_element_type=F32)
        sums += [both[:, :LANE], both[:, LANE:]]
    for t in range(SNAP):
        for z in range(n_zone):
            part = sums[t][z * BLOCKS : (z + 1) * BLOCKS]
            part_out[z, t] = part.astype(BF16)
            part_own[z, t] = part
    p_copies = []
    for n, peer in enumerate(zones):
        p_copies.append(
            pltpu.make_async_remote_copy(
                src_ref=part_out.at[peer],
                dst_ref=part_in.at[n],
                send_sem=p_send.at[n],
                recv_sem=p_recv.at[n],
                device_id={"zone": peer},
                device_id_type=MESH,
            )
        )
        p_copies[-1].start()
    for copy in x_copies:
        copy.wait_send()
    rows_wait_owners(send_a, a_send)

    @pl.when(owner)
    def _():
        rows_wait(send_b, 2 * n_tm - 2, b_send)

    for copy in p_copies:
        copy.wait_recv()
    for t in range(SNAP):
        total = part_own[zone, t]
        for n in range(n_zone - 1):
            total += part_in[n, t].astype(F32)
        arranged[pl.ds(t, BLOCKS, stride=SNAP), :] = total
    for i in range(BLOCKS):
        out[:, i * LANE : (i + 1) * LANE] = arranged[i * SNAP : (i + 1) * SNAP, :]
    for copy in p_copies:
        copy.wait_send()


def solution(mesh):
    n_tm, n_zone = mesh.shape["tm"], mesh.shape["zone"]

    def shards(source_field, remap_weights, block_columns, piece_sizes, filter_taps):
        hbm = pl.BlockSpec(memory_space=pltpu.HBM)
        vmem = pl.BlockSpec(memory_space=pltpu.VMEM)
        dma = pltpu.SemaphoreType.DMA
        return pl.pallas_call(
            functools.partial(kernel, n_tm, n_zone),
            name="flux",
            out_shape=pltpu.VMEM(source_field.shape, F32),
            in_specs=[hbm] * 5,
            out_specs=vmem,
            scratch_shapes=[
                pltpu.VMEM(source_field.shape, F32),
                pltpu.VMEM((BLOCKS * n_zone, SNAP, LANE), BF16),
                pltpu.VMEM(remap_weights.shape, BF16),
                pltpu.VMEM((BLOCKS, SLOTS * LANE, LANE), BF16),
                pltpu.SMEM((SLOTS, BLOCKS), jnp.int32),
                pltpu.VMEM(piece_sizes.shape, jnp.int32),
                pltpu.VMEM(filter_taps.shape, F32),
                [pltpu.VMEM((len(BANDS) * len(slab) * 16, 512), BF16) for slab in SLABS],
                pltpu.VMEM((LANE, BLOCKS * LANE), BF16),
                pltpu.VMEM((BLOCKS * LANE, LANE), BF16),
                pltpu.VMEM((n_tm, LANE), F32),
                pltpu.VMEM((2 * n_tm, LANE), F32),
                pltpu.VMEM((2 * n_tm, LANE), BF16),
                pltpu.VMEM((n_tm, LANE), BF16),
                pltpu.VMEM((2 * n_tm, LANE), F32),
                pltpu.VMEM((BLOCKS * SLOTS * SNAP, LANE), F32),
                pltpu.VMEM((n_zone, SNAP, BLOCKS, LANE), BF16),
                pltpu.VMEM((n_zone - 1, SNAP, BLOCKS, LANE), BF16),
                pltpu.VMEM((n_zone, SNAP, BLOCKS, LANE), F32),
                pltpu.VMEM((BLOCKS * SNAP, LANE), F32),
                dma((5,)),
                dma((n_zone - 1,)),
                dma((n_zone - 1,)),
                dma,
                dma,
                dma,
                dma((4,)),
                dma((n_zone - 1,)),
                dma((n_zone - 1,)),
                pltpu.SemaphoreType.REGULAR((4,)),
            ],
            compiler_params=pltpu.CompilerParams(collective_id=0, has_side_effects=True),
        )(source_field, remap_weights, block_columns.T, piece_sizes, filter_taps)

    return jax.shard_map(
        shards,
        mesh=mesh,
        in_specs=(
            P("tm", "zone"),
            P("zone", None, None, None),
            P("zone", None),
            P("zone", None),
            P(),
        ),
        out_specs=P("tm", "zone"),
        check_vma=False,
    )
```

```python
import functools

import jax
import jax.numpy as jnp
from jax import lax
from jax.experimental import pallas as pl
from jax.experimental.pallas import tpu as pltpu
from jax.sharding import PartitionSpec as P

MESH = pl.DeviceIdType.MESH
F32 = jnp.float32
BF16 = jnp.bfloat16
SNAP = 8
LANE = 128
BLOCKS = 16
SLOTS = 8
SLABS = [(0,), (1, 2), (3, 4, 5, 6, 7)]
BANDS = [(0, 0), (0, 1)] + [(g, u) for g in (1, 2, 3) for u in (0, 1, 2)]


def iota(shape, dim):
    return lax.broadcasted_iota(jnp.int32, shape, dim)


def two_parts(value):
    high = value.astype(BF16)
    low = (value - high.astype(F32)).astype(BF16)
    return high, low


def ring_distance(offset, length):
    return min(offset, length - offset)


def kernel(
    n_tm,
    n_zone,
    source,
    weights,
    columns,
    sizes,
    taps,
    out,
    x_in,
    x_all,
    w_all,
    w_turned,
    cols,
    size_in,
    tap_in,
    toeplitz,
    members,
    members_tall,
    send_a,
    recv_a,
    send_b,
    recv_b,
    paired,
    contrib,
    part_out,
    part_in,
    part_own,
    arranged,
    load_sem,
    x_send,
    x_recv,
    a_send,
    a_recv,
    b_send,
    b_recv,
    p_send,
    p_recv,
    word,
):
    tm = lax.axis_index("tm")
    zone = lax.axis_index("zone")
    rings, ring, cores = 8, 8, 2
    span = ring * cores
    owners = n_tm // 2
    tz, tq = tm // span, lax.rem(tm, span)
    owner = tm < owners
    sides = sorted(range(span), key=lambda dq: -ring_distance(dq // cores, ring))
    zones = [lax.rem(zone + step, n_zone) for step in (2, 1, 3)]

    core = lax.rem(tq, cores)

    def beside(step):
        return tz * span + lax.rem(tq + step * cores + span, span)

    def greet(semaphore, peer):
        pl.semaphore_signal(semaphore, inc=1, device_id={"tm": peer}, device_id_type=MESH)

    zone_order = [
        jnp.where(zone == 2, 1, 2),
        jnp.where((zone == 1) | (zone == 2), 3, 1),
        jnp.where(zone == 0, 3, 0),
    ]

    barrier = pltpu.get_barrier_semaphore()
    for peer in zones:
        pl.semaphore_signal(barrier, inc=1, device_id={"zone": peer}, device_id_type=MESH)
    lines = [lax.rem(tz + dz, 4) * span + tq for dz in (1, 2, 3)]
    host = jnp.where(tz < 6, 3, 0) * span + tq
    hosting = (tz == 0) | (tz == 3)
    guests = [jnp.where(tz == 0, far, near) * span + tq for far, near in ((7, 4), (6, 5))]

    @pl.when(owner)
    def _():
        for step in (2, -2, 1, -1):
            greet(barrier, beside(step))
            greet(barrier, beside(step) + 1 - 2 * core)
        greet(barrier, tm + 1 - 2 * core)
        for peer in lines:
            greet(barrier, peer)

    @pl.when(hosting)
    def _():
        for peer in guests:
            greet(barrier, peer)

    load_x = pltpu.make_async_copy(source, x_in, load_sem.at[0])
    load_c = pltpu.make_async_copy(columns, cols, load_sem.at[1])
    load_w = pltpu.make_async_copy(weights, w_all, load_sem.at[2])
    load_s = pltpu.make_async_copy(sizes, size_in, load_sem.at[3])
    load_t = pltpu.make_async_copy(taps, tap_in, load_sem.at[4])
    for load in (load_x, load_c, load_s, load_w, load_t):
        load.start()

    load_x.wait()
    for i in range(BLOCKS):
        x_all[zone * BLOCKS + i] = x_in[:, i * LANE : (i + 1) * LANE].astype(BF16)
    pl.semaphore_wait(barrier, n_zone - 1 + jnp.where(owner, 12, 1))
    mine = x_all.at[pl.ds(zone * BLOCKS, BLOCKS)]
    x_copies = []
    for peer in zone_order:
        step = lax.rem(peer - zone + n_zone, n_zone) - 1
        x_copies.append(
            pltpu.make_async_remote_copy(
                src_ref=mine,
                dst_ref=mine,
                send_sem=x_send.at[step],
                recv_sem=x_recv.at[step],
                device_id={"zone": peer},
                device_id_type=MESH,
            )
        )
        x_copies[-1].start()

    @pl.when(owner)
    def _():
        for step in (2, -2):
            greet(word.at[0], beside(step))

    @pl.when(jnp.logical_not(owner))
    def _():
        greet(word.at[2], host)

    load_s.wait()
    size_row = size_in[...].astype(F32)
    down, along = iota((LANE, LANE), 0), iota((LANE, LANE), 1)
    size_wide = jnp.broadcast_to(size_row, (LANE, LANE))
    size_tall = size_wide.T
    upto = jnp.sum(jnp.where(along <= down, size_wide, 0.0), axis=1, keepdims=True)
    before = jnp.sum(jnp.where(along < down, size_wide, 0.0), axis=1, keepdims=True)
    upto_row = jnp.sum(jnp.where(down <= along, size_tall, 0.0), axis=0, keepdims=True)
    before_row = jnp.sum(jnp.where(down < along, size_tall, 0.0), axis=0, keepdims=True)
    for i in range(BLOCKS):
        cell = (along + i * LANE).astype(F32)
        inside = (cell >= before) & (cell < upto)
        members[:, i * LANE : (i + 1) * LANE] = inside.astype(BF16)
        cell = (down + i * LANE).astype(F32)
        inside = (cell >= before_row) & (cell < upto_row)
        members_tall[i * LANE : (i + 1) * LANE, :] = inside.astype(BF16)

    @pl.when(owner)
    def _():
        pl.semaphore_wait(word.at[0], 2)
        for peer in lines:
            greet(word.at[1], peer)

    load_t.wait()
    load_c.wait()
    load_w.wait()
    for i in range(BLOCKS):
        for k in range(SLOTS):
            w_turned[i, k * LANE : (k + 1) * LANE, :] = w_all[i, k].T
    for copy in x_copies:
        copy.wait_recv()

    @pl.when(owner)
    def _():
        pl.semaphore_wait(word.at[1], 3)

    @pl.when(hosting)
    def _():
        pl.semaphore_wait(word.at[2], 2)
        for peer in guests:
            greet(word.at[3], peer)

    stress = []
    for i in range(BLOCKS):
        picked = jnp.concatenate([x_all[cols[k, i]] for k in range(SLOTS)], axis=1)
        wind = jnp.dot(picked, w_turned[i], preferred_element_type=F32)
        stress.append(wind * jnp.abs(wind))

    wide = jnp.concatenate(stress, axis=1)
    high, low = two_parts(wide)
    both = jnp.concatenate([high, low], axis=0)
    totals = jnp.dot(both, members_tall[...], preferred_element_type=F32)
    means = (totals[:SNAP] + totals[SNAP:]) / size_row
    high, low = two_parts(means)
    both = jnp.concatenate([high, low], axis=0)
    spread = jnp.dot(both, members[...], preferred_element_type=F32)
    anomaly = wide - spread[:SNAP] - spread[SNAP:]
    tiles = jnp.concatenate([anomaly[:, i * LANE : (i + 1) * LANE] for i in range(BLOCKS)], axis=0)

    def rows_wait(ref, rows, sem):
        part = ref.at[pl.ds(0, rows)]
        pltpu.make_async_copy(part, part, sem).wait()

    def rows_wait_owners(ref, sem):
        @pl.when(owner)
        def _():
            rows_wait(ref, 2 * owners - 2, sem)

        @pl.when(jnp.logical_not(owner))
        def _():
            rows_wait(ref, 2 * owners, sem)

    turned = tiles.T
    first, second = turned[:owners], turned[owners:]
    odd = lax.rem(iota((owners, LANE), 1) // 4, 2) == 1
    send_a[pl.ds(0, owners, stride=2), :] = jnp.where(odd, pltpu.roll(second, 4, 1), first)
    send_a[pl.ds(1, owners, stride=2), :] = jnp.where(odd, second, pltpu.roll(first, LANE - 4, 1))

    def send_row(peer):
        pltpu.make_async_remote_copy(
            src_ref=send_a.at[pl.ds(2 * peer, 2)],
            dst_ref=recv_a.at[pl.ds(2 * tm, 2)],
            send_sem=a_send,
            recv_sem=a_recv,
            device_id={"tm": peer},
            device_id_type=MESH,
        ).start()

    steps = [(j, dq) for j in range(4) for dq in range(span)]
    steps.sort(key=lambda step: -((4, 3, 2, 3)[step[0]] + ring_distance(step[1] // cores, ring)))

    @pl.when(jnp.logical_not(owner))
    def _():
        pl.semaphore_wait(word.at[3], 1)

    for j, dq in steps:
        peer = lax.rem(tz + j, 4) * span + lax.rem(tq + dq, span)
        if j == 0 and dq == 0:
            pl.when(jnp.logical_not(owner))(functools.partial(send_row, peer))
        else:
            send_row(peer)

    @pl.when(owner)
    def _():
        recv_a[pl.ds(2 * tm, 2)] = send_a[pl.ds(2 * tm, 2)]

        pieces = []
        for q in range(8):
            row = tap_in[pl.ds(q * LANE - q // 7, LANE)].reshape(1, LANE)
            if q == 7:
                row = jnp.where(iota((1, LANE), 1) < LANE - 1, pltpu.roll(row, LANE - 1, 1), 0.0)
            row = jnp.broadcast_to(row, (8, LANE))
            pieces.append(jnp.where(lax.rem(iota((8, LANE), 1), 4) == iota((8, LANE), 0), row, 0.0))
        spread = jnp.concatenate(pieces, axis=1)
        pick = (iota((1024, 256), 0) // 4 == iota((1024, 256), 1)).astype(BF16)
        top, rest = two_parts(spread)
        last = (spread - top.astype(F32) - rest.astype(F32)).astype(BF16)
        by_phase = (
            jnp.dot(top, pick, preferred_element_type=F32)
            + jnp.dot(rest, pick, preferred_element_type=F32)
            + jnp.dot(last, pick, preferred_element_type=F32)
        )
        for n, (g, u) in enumerate(BANDS):
            phase, start = (3, 127) if g == 0 else (g - 1, 128)
            line = jnp.concatenate([by_phase[phase : phase + 1, :], jnp.zeros((1, 256), F32)], axis=1)
            wide = jnp.broadcast_to(line, (LANE, 512))
            high, low = two_parts(pltpu.roll(wide, (u - start) % 512, 1, stride=2, stride_axis=0)[:, :256])
            for slab, ref in zip(SLABS, toeplitz):
                rows, base = len(slab) * span, slab[0] * span
                ref[n * rows : (n + 1) * rows, :256] = high[base : base + rows]
                ref[n * rows : (n + 1) * rows, 256:] = low[base : base + rows]
        rows_wait(recv_a, 2 * n_tm - 2, a_recv)

        high, low = two_parts(recv_a[...])
        upper = jnp.concatenate([high, low], axis=1)
        lower = jnp.concatenate([high, jnp.zeros_like(high)], axis=1)
        right = jnp.concatenate([upper, lower], axis=0)

        def send_back(peer):
            pltpu.make_async_remote_copy(
                src_ref=send_b.at[pl.ds(2 * peer, 2)],
                dst_ref=recv_b.at[pl.ds(2 * tm, 2)],
                send_sem=b_send,
                recv_sem=b_recv.at[tz],
                device_id={"tm": peer},
                device_id_type=MESH,
            ).start()

        for slab, ref in zip(SLABS, toeplitz):
            rows, base = len(slab) * span, slab[0] * span
            place = lax.rem(iota((rows, LANE), 1), 4)
            product = jnp.dot(ref[...], right, preferred_element_type=F32)
            product = product[:, :LANE] + product[:, LANE:]
            band = {b: product[n * rows : (n + 1) * rows] for n, b in enumerate(BANDS)}
            for u in range(2):
                total = band[0, u]
                for g in (1, 2, 3):
                    total += jnp.where(
                        place < 4 - g,
                        pltpu.roll(band[g, u], LANE - g, 1),
                        pltpu.roll(band[g, u + 1], 4 - g, 1),
                    )
                paired[pl.ds(2 * base + u, rows, stride=2), :] = total
            send_b[2 * base : 2 * (base + rows), :] = paired[2 * base : 2 * (base + rows), :].astype(BF16)
            for z in slab:
                for dq in sides:
                    peer = z * span + lax.rem(tq + dq, span)
                    if z < rings // 2 and dq == 0:
                        pl.when(tz != z)(functools.partial(send_back, peer))
                    else:
                        send_back(peer)
        here = pl.ds(2 * tm, 2)
        own = pltpu.make_async_copy(send_b.at[here], recv_b.at[here], load_sem.at[0])
        own.start()
        own.wait()

    n_pairs = BLOCKS * SLOTS
    all_blocks = BLOCKS * n_zone
    column_row = jnp.zeros((1, LANE), jnp.int32)
    lane = iota((1, LANE), 1)
    for i in range(BLOCKS):
        for k in range(SLOTS):
            column_row = jnp.where(lane == i * SLOTS + k, cols[k, i], column_row)
    chosen = (iota((all_blocks, LANE), 0) == column_row).astype(BF16)
    chosen = jnp.concatenate([chosen, chosen], axis=1)

    quarter = owners // 4
    strip = 2 * quarter
    odd = lax.rem(iota((quarter, LANE), 1) // 4, 2) == 1
    for part in range(4):
        mine_too = tz == part
        from_rows = recv_b.at[pl.ds(strip * part, strip)]
        but_mine = recv_b.at[pl.ds(strip * part, strip - 2)]

        @pl.when(mine_too)
        def _():
            pltpu.make_async_copy(but_mine, but_mine, b_recv.at[part]).wait()

        @pl.when(jnp.logical_not(mine_too))
        def _():
            pltpu.make_async_copy(from_rows, from_rows, b_recv.at[part]).wait()

        paired[part * strip : (part + 1) * strip, :] = recv_b[part * strip : (part + 1) * strip, :].astype(F32)
        even_row = paired[pl.ds(part * strip, quarter, stride=2), :]
        odd_row = paired[pl.ds(part * strip + 1, quarter, stride=2), :]
        first = jnp.where(odd, pltpu.roll(odd_row, 4, 1), even_row)
        second = jnp.where(odd, odd_row, pltpu.roll(even_row, LANE - 4, 1))
        flow = jnp.concatenate([first, second], axis=0).T.astype(BF16)
        low_a, high_a = part * quarter, owners + part * quarter
        for i in range(BLOCKS):
            left = flow[i * SNAP : (i + 1) * SNAP, :]
            for k in range(0, SLOTS, 2):
                w_low = [w_all[i, n, low_a : low_a + quarter, :] for n in (k, k + 1)]
                w_high = [w_all[i, n, high_a : high_a + quarter, :] for n in (k, k + 1)]
                w_pair = jnp.concatenate(
                    [jnp.concatenate(w_low, axis=1), jnp.concatenate(w_high, axis=1)], axis=0
                )
                pair = jnp.dot(left, w_pair, preferred_element_type=F32)
                for n in range(2):
                    base = (i * SLOTS + k + n) * SNAP
                    term = pair[:, n * LANE : (n + 1) * LANE]
                    if part == 0:
                        contrib[base : base + SNAP, :] = term
                    else:
                        contrib[base : base + SNAP, :] += term
    sums = []
    for t in range(0, SNAP, 2):
        sides = []
        for side in (t, t + 1):
            high, low = two_parts(contrib[pl.ds(side, n_pairs, stride=SNAP), :])
            sides.append(jnp.concatenate([high, low], axis=0))
        both = jnp.dot(chosen, jnp.concatenate(sides, axis=1), preferred_element_type=F32)
        sums += [both[:, :LANE], both[:, LANE:]]
    for t in range(SNAP):
        for z in range(n_zone):
            part = sums[t][z * BLOCKS : (z + 1) * BLOCKS]
            part_out[z, t] = part.astype(BF16)
            part_own[z, t] = part
    p_copies = []
    for n, peer in enumerate(zones):
        p_copies.append(
            pltpu.make_async_remote_copy(
                src_ref=part_out.at[peer],
                dst_ref=part_in.at[n],
                send_sem=p_send.at[n],
                recv_sem=p_recv.at[n],
                device_id={"zone": peer},
                device_id_type=MESH,
            )
        )
        p_copies[-1].start()
    for copy in x_copies:
        copy.wait_send()
    rows_wait_owners(send_a, a_send)

    @pl.when(owner)
    def _():
        rows_wait(send_b, 2 * n_tm - 2, b_send)

    for copy in p_copies:
        copy.wait_recv()
    for t in range(SNAP):
        total = part_own[zone, t]
        for n in range(n_zone - 1):
            total += part_in[n, t].astype(F32)
        arranged[pl.ds(t, BLOCKS, stride=SNAP), :] = total
    for i in range(BLOCKS):
        out[:, i * LANE : (i + 1) * LANE] = arranged[i * SNAP : (i + 1) * SNAP, :]
    for copy in p_copies:
        copy.wait_send()


def solution(mesh):
    n_tm, n_zone = mesh.shape["tm"], mesh.shape["zone"]

    def shards(source_field, remap_weights, block_columns, piece_sizes, filter_taps):
        hbm = pl.BlockSpec(memory_space=pltpu.HBM)
        vmem = pl.BlockSpec(memory_space=pltpu.VMEM)
        dma = pltpu.SemaphoreType.DMA
        return pl.pallas_call(
            functools.partial(kernel, n_tm, n_zone),
            name="flux",
            out_shape=pltpu.VMEM(source_field.shape, F32),
            in_specs=[hbm] * 5,
            out_specs=vmem,
            scratch_shapes=[
                pltpu.VMEM(source_field.shape, F32),
                pltpu.VMEM((BLOCKS * n_zone, SNAP, LANE), BF16),
                pltpu.VMEM(remap_weights.shape, BF16),
                pltpu.VMEM((BLOCKS, SLOTS * LANE, LANE), BF16),
                pltpu.SMEM((SLOTS, BLOCKS), jnp.int32),
                pltpu.VMEM(piece_sizes.shape, jnp.int32),
                pltpu.VMEM(filter_taps.shape, F32),
                [pltpu.VMEM((len(BANDS) * len(slab) * 16, 512), BF16) for slab in SLABS],
                pltpu.VMEM((LANE, BLOCKS * LANE), BF16),
                pltpu.VMEM((BLOCKS * LANE, LANE), BF16),
                pltpu.VMEM((n_tm, LANE), F32),
                pltpu.VMEM((2 * n_tm, LANE), F32),
                pltpu.VMEM((2 * n_tm, LANE), BF16),
                pltpu.VMEM((n_tm, LANE), BF16),
                pltpu.VMEM((2 * n_tm, LANE), F32),
                pltpu.VMEM((BLOCKS * SLOTS * SNAP, LANE), F32),
                pltpu.VMEM((n_zone, SNAP, BLOCKS, LANE), BF16),
                pltpu.VMEM((n_zone - 1, SNAP, BLOCKS, LANE), BF16),
                pltpu.VMEM((n_zone, SNAP, BLOCKS, LANE), F32),
                pltpu.VMEM((BLOCKS * SNAP, LANE), F32),
                dma((5,)),
                dma((n_zone - 1,)),
                dma((n_zone - 1,)),
                dma,
                dma,
                dma,
                dma((4,)),
                dma((n_zone - 1,)),
                dma((n_zone - 1,)),
                pltpu.SemaphoreType.REGULAR((4,)),
            ],
            compiler_params=pltpu.CompilerParams(collective_id=0, has_side_effects=True),
        )(source_field, remap_weights, block_columns.T, piece_sizes, filter_taps)

    return jax.shard_map(
        shards,
        mesh=mesh,
        in_specs=(
            P("tm", "zone"),
            P("zone", None, None, None),
            P("zone", None),
            P("zone", None),
            P(),
        ),
        out_specs=P("tm", "zone"),
        check_vma=False,
    )
```
